256 devices in a mesh: group: 16 (over y, x_hi, core), tile: 16 (over x_lo, z).
Axes of the slice: x: 4 (x_hi: 2, x_lo: 2; x = x_hi * 2 + x_lo), y: 4, z: 8, core: 2. Of those that a mesh axis runs over, the one named last changes fastest.
Arguments:
- coupling: float32 [64, 1024, 768], P('group', None, 'tile'), may hold values from -6 to 6
- interior_solve: float32 [64, 768, 1024], P('group', 'tile'), may hold values from -0.21875 to 0.21875
- boundary_stiffness: float32 [64, 1024, 1024], P('group', 'tile'), may hold values from -6 to 6
- migration: int32 [64], replicated, may hold values from -1 to 31, as said below
Outputs:
- condensed: float32 [32, 1024, 1024], P('group', 'tile')
The draws below stay inside these ranges and needn't reach their ends.
Inputs may be any that keep to these rules, and one draw needn't show every extreme that they name: `migration`: every condensed slot is named by exactly one RVE slot; RVE slots of group g are g * 4 to g * 4 + 3; the condensed slots of group g are named only by RVE slots of group g or of its partner, the group whose index differs from g in the lowest bit; some group holds 4 plastic RVEs.
All inputs are finite; a program needn't handle non-finite values.
Results may differ from the reference program's by a relative error of at most 0.000071.
Values sent between devices are 32-bit elements; how exact they have to be, the bound alone decides.
No kernel may reach another device: no remote copies, remote signals or barrier semaphores. Data moves between devices by JAX's collectives and lax.ppermute only.
A program may use at most 64 MiB of HBM per device.

```python
import jax
import jax.numpy as jnp
from jax import lax

BOUNDARY = 1024
INTERIOR = 768
OWN = 2
HOME = 4
RVES = 64
SLOTS = 32


def draw_migration(key, part):
    groups = RVES // HOME
    couples = groups // 2
    key_heavy, key_slots = jax.random.split(jax.random.fold_in(key, 23))
    heavy_bit = jax.random.randint(key_heavy, (couples,), 0, 2).astype(jnp.int32)
    couple_ids = jnp.arange(couples, dtype=jnp.int32)
    heavies = 2 * couple_ids + heavy_bit
    lights = 2 * couple_ids + 1 - heavy_bit
    slot_ids = jnp.arange(OWN, dtype=jnp.int32)[None, :]
    targets = jnp.concatenate([heavies[:, None] * OWN + slot_ids, lights[:, None] * OWN + slot_ids], axis=1)
    subkeys = jax.random.split(key_slots, couples)
    shuffles = jax.vmap(lambda sub_key: jax.random.permutation(sub_key, HOME))(subkeys).astype(jnp.int32)
    places = heavies[:, None] * HOME + shuffles
    result = jnp.full((RVES,), -1, jnp.int32)
    return result.at[places.reshape(-1)].set(targets.reshape(-1).astype(jnp.int32))


def block_scale(key, extent, shards, least, largest):
    level = 1.0
    for dim, parts in shards:
        steps = jax.random.uniform(jax.random.fold_in(jax.random.fold_in(key, 6), dim), (parts,), jnp.float32, least / len(shards), largest / len(shards))
        level = level * jnp.repeat(jnp.exp(steps), extent[dim] // parts).reshape((-1,) + (1,) * (len(extent) - 1 - dim))
    return level


def scatter_about(rng, dims, spread, bound, cuts=(), kind=jnp.bfloat16):
    drawn = spread * jax.random.normal(rng, dims, jnp.float32)
    if cuts:
        drawn = drawn * block_scale(rng, dims, cuts, -0.22, 0.18)
    return jnp.clip(drawn, -bound, bound).astype(kind)


def setup_inputs(seed: int = 0) -> dict:
    arg_keys = jax.random.split(jax.random.key(seed), 5)
    return {
        "coupling": scatter_about(arg_keys[0], (RVES, BOUNDARY, INTERIOR), 1.0, 6.0, ((0, 16), (2, 16)), jnp.float32),
        "interior_solve": scatter_about(arg_keys[1], (RVES, INTERIOR, BOUNDARY), INTERIOR ** -0.5, 0.21875, ((0, 16), (1, 16)), jnp.float32),
        "boundary_stiffness": scatter_about(arg_keys[2], (RVES, BOUNDARY, BOUNDARY), 1.0, 6.0, ((0, 16), (1, 16)), jnp.float32),
        "migration": draw_migration(jax.random.fold_in(arg_keys[4], 71), 0),
    }


def reference(coupling, interior_solve, boundary_stiffness, migration):
    targets = jnp.where(migration >= 0, migration, SLOTS).astype(jnp.int32)
    sources = jnp.zeros((SLOTS,), jnp.int32).at[targets].set(jnp.arange(RVES, dtype=jnp.int32), mode="drop")

    def condense_one(source):
        product = jnp.dot(coupling[source], interior_solve[source], precision=lax.Precision.HIGHEST, preferred_element_type=jnp.float32)
        return boundary_stiffness[source] - product

    return lax.map(condense_one, sources)
```

```python
import jax
import jax.numpy as jnp
from jax import lax
from jax.experimental import pallas as pl
from jax.experimental.pallas import tpu as pltpu
from jax.sharding import Mesh
from jax.sharding import PartitionSpec as P

OWN = 2
TILE = ("tile_0", "tile_1")
LANES = 128
PARAMS = pltpu.CompilerParams(vmem_limit_bytes=32 * 1024 * 1024)
SMEM = pl.BlockSpec(memory_space=pltpu.SMEM)
VMEM = pl.BlockSpec(memory_space=pltpu.VMEM)
HBM = pl.BlockSpec(memory_space=pltpu.HBM)


def hops(slot):
    return (4, 3) if slot == 0 else (3, 4)


def locate(plan, group, wanted, home):
    position, here = jnp.int32(0), jnp.bool_(False)
    for k in range(home):
        match = plan[group * home + k] == wanted
        position = jnp.where(match, jnp.int32(k), position)
        here = jnp.logical_or(here, match)
    return position, here


def pack(plan, coupling, solve, for_partner):
    home, depth, width = solve.shape
    blocks = width // LANES

    def kernel(plan_ref, c_hbm, x_hbm, out0, out1, c_buf, x_sem, c_sem):
        group = lax.axis_index("group")
        place = lax.axis_index("tile_1")
        owner = jnp.bitwise_xor(group, 1) if for_partner else group
        outs = (out0, out1)
        copies = []
        for slot in range(OWN):
            position, _ = locate(plan_ref, group, owner * OWN + slot, home)
            c_copy = pltpu.make_async_copy(c_hbm.at[position], c_buf.at[slot], c_sem.at[slot])
            c_copy.start()
            x_copies = []
            up = hops(slot)[0]
            for n in range(blocks):
                x_copy = pltpu.make_async_copy(
                    x_hbm.at[position, :, pl.ds(n * LANES, LANES)], outs[slot].at[up + n], x_sem.at[slot, n]
                )
                x_copy.start()
                x_copies.append(x_copy)
            copies.append((c_copy, x_copies))
        low = lax.broadcasted_iota(jnp.int32, (depth, LANES), 1) < LANES // 2
        for slot in range(OWN):
            c_copy, x_copies = copies[slot]
            up = hops(slot)[0]
            c_copy.wait()
            for m in range(blocks // 2):
                first = c_buf[slot, :, pl.ds(m * LANES, LANES)]
                second = c_buf[slot, :, pl.ds((m + blocks // 2) * LANES, LANES)]
                even = jnp.where(low, first, pltpu.roll(second, LANES // 2, 1))
                odd = jnp.where(low, pltpu.roll(first, LANES // 2, 1), second)
                for to, piece in ((2 * m, even), (2 * m + 1, odd)):
                    ahead = jnp.bitwise_and(to - place, blocks - 1)
                    spot = jnp.where(ahead == 0, 15, jnp.where(ahead <= up, ahead - 1, ahead + 7))
                    outs[slot][spot] = piece
            for x_copy in x_copies:
                x_copy.wait()

    packet = jax.ShapeDtypeStruct((2 * blocks, depth, LANES), jnp.float32)
    return pl.pallas_call(
        kernel,
        out_shape=(packet, packet),
        in_specs=[SMEM, HBM, HBM],
        out_specs=(VMEM, VMEM),
        scratch_shapes=[
            pltpu.VMEM((OWN, depth, width), jnp.float32),
            pltpu.SemaphoreType.DMA((OWN, blocks)),
            pltpu.SemaphoreType.DMA((OWN,)),
        ],
        compiler_params=PARAMS,
        name="pack_partner" if for_partner else "pack_own",
    )(plan, coupling, solve)


def merge(plan, arrived, local, slot, home):
    total, depth, _ = arrived.shape
    up, down = hops(slot)
    blocks = total // 2

    def kernel(plan_ref, arrived_ref, local_ref, up_ref, down_ref, own_ref):
        group = lax.axis_index("group")
        _, here = locate(plan_ref, group, group * OWN + slot, home)

        def put(source):
            up_ref[...] = source[0 : up + blocks]
            down_ref[...] = source[up : total - 1]
            own_ref[...] = source[total - 1]

        @pl.when(here)
        def _():
            put(local_ref)

        @pl.when(jnp.logical_not(here))
        def _():
            put(arrived_ref)

    return pl.pallas_call(
        kernel,
        out_shape=(
            jax.ShapeDtypeStruct((up + blocks, depth, LANES), jnp.float32),
            jax.ShapeDtypeStruct((down + blocks, depth, LANES), jnp.float32),
            jax.ShapeDtypeStruct((depth, LANES), jnp.float32),
        ),
        in_specs=[SMEM, VMEM, VMEM],
        out_specs=(VMEM, VMEM, VMEM),
        compiler_params=PARAMS,
        name=f"merge_{slot}",
    )(plan, arrived, local)


def stiff_out(plan, stiff):
    home, rows, width = stiff.shape

    def kernel(plan_ref, b_hbm, out_ref, sem):
        group = lax.axis_index("group")
        copies = []
        for slot in range(OWN):
            position, _ = locate(plan_ref, group, jnp.bitwise_xor(group, 1) * OWN + slot, home)
            copy = pltpu.make_async_copy(b_hbm.at[position], out_ref.at[slot], sem.at[slot])
            copy.start()
            copies.append(copy)
        for copy in copies:
            copy.wait()

    return pl.pallas_call(
        kernel,
        out_shape=jax.ShapeDtypeStruct((OWN, rows, width), jnp.float32),
        in_specs=[SMEM, HBM],
        out_specs=VMEM,
        scratch_shapes=[pltpu.SemaphoreType.DMA((OWN,))],
        compiler_params=PARAMS,
        name="stiff_out",
    )(plan, stiff)


def stiff_merge(plan, stiff, arrived):
    home, rows, width = stiff.shape

    def kernel(plan_ref, b_hbm, arrived_ref, out_ref, sem):
        group = lax.axis_index("group")
        for slot in range(OWN):
            position, here = locate(plan_ref, group, group * OWN + slot, home)

            @pl.when(here)
            def _():
                copy = pltpu.make_async_copy(b_hbm.at[position], out_ref.at[slot], sem.at[slot])
                copy.start()
                copy.wait()

            @pl.when(jnp.logical_not(here))
            def _():
                out_ref[slot] = arrived_ref[slot]

    return pl.pallas_call(
        kernel,
        out_shape=jax.ShapeDtypeStruct((OWN, rows, width), jnp.float32),
        in_specs=[SMEM, HBM, VMEM],
        out_specs=VMEM,
        scratch_shapes=[pltpu.SemaphoreType.DMA((OWN,))],
        compiler_params=PARAMS,
        name="stiff_merge",
    )(plan, stiff, arrived)


def split(value):
    high = value.astype(jnp.bfloat16)
    return high, (value - high.astype(jnp.float32)).astype(jnp.bfloat16)


def add_chunks(total_ref, chunks, start):
    width = total_ref.shape[1]
    pairs = width // (2 * LANES)
    for packet, first, piece in chunks:
        c_high, c_low = split(piece)
        left = jnp.concatenate([c_high, c_high, c_low], axis=0)
        for n in range(pairs):
            x = jnp.concatenate([packet[first + 2 * n], packet[first + 2 * n + 1]], axis=1)
            x_high, x_low = split(x)
            right = jnp.concatenate([x_high, x_low, x_high], axis=0)
            product = lax.dot_general(left, right, (((0,), (0,)), ((), ())), preferred_element_type=jnp.float32)
            where = (slice(None), pl.ds(2 * n * LANES, 2 * LANES))
            total_ref[where] = product if start else total_ref[where] + product
        start = False


def accumulate(total, sources, width, name):
    packets = []
    layout = []
    for packet, first, piece in sources:
        packets.append(packet)
        if isinstance(piece, int):
            layout.append((len(packets) - 1, first, None, piece))
        else:
            packets.append(piece)
            layout.append((len(packets) - 2, first, len(packets) - 1, None))
    given = [] if total is None else [total]
    n_given = len(given)

    def kernel(*refs):
        total_ref = refs[-1]
        ins = refs[n_given:-1]
        if n_given:
            total_ref[...] = refs[0][...]
        chunks = [
            (ins[k], first, ins[own][...] if own is not None else ins[k][index]) for k, first, own, index in layout
        ]
        add_chunks(total_ref, chunks, not n_given)

    return pl.pallas_call(
        kernel,
        out_shape=jax.ShapeDtypeStruct((LANES, width), jnp.float32),
        in_specs=[VMEM] * (n_given + len(packets)),
        out_specs=VMEM,
        input_output_aliases={0: 0} if n_given else {},
        compiler_params=PARAMS,
        cost_estimate=pl.CostEstimate(flops=2 * 144 * 128 * 1024, bytes_accessed=1 << 20, transcendentals=0),
        name=name,
    )(*given, *packets)


def last_chunk(total, packet, first, index, stiff, slot, name):
    rows, width = LANES // 2, total.shape[1]

    def kernel(total_ref, packet_ref, stiff_ref, send_ref, keep_ref, sum_ref):
        sum_ref[...] = total_ref[...]
        add_chunks(sum_ref, [(packet_ref, first, packet_ref[index])], False)
        mine = lax.axis_index("tile_0")
        send_ref[...] = sum_ref[pl.ds(pl.multiple_of((1 - mine) * rows, rows), rows), :]
        keep_ref[...] = stiff_ref[slot] - sum_ref[pl.ds(pl.multiple_of(mine * rows, rows), rows), :]

    half = jax.ShapeDtypeStruct((rows, width), jnp.float32)
    return pl.pallas_call(
        kernel,
        out_shape=(half, half),
        in_specs=[VMEM] * 3,
        out_specs=(VMEM, VMEM),
        scratch_shapes=[pltpu.VMEM((LANES, width), jnp.float32)],
        compiler_params=PARAMS,
        name=name,
    )(total, packet, stiff)


def finish(keeps, others):
    rows, width = keeps[0].shape

    def kernel(k0, k1, o0, o1, out_ref):
        out_ref[0] = k0[...] - o0[...]
        out_ref[1] = k1[...] - o1[...]

    return pl.pallas_call(
        kernel,
        out_shape=jax.ShapeDtypeStruct((OWN, rows, width), jnp.float32),
        in_specs=[VMEM] * 4,
        out_specs=VMEM,
        compiler_params=PARAMS,
        name="finish",
    )(*keeps, *others)


def shifted(array, axis, distance):
    size = lax.axis_size(axis)
    return lax.ppermute(array, axis, [(i, (i + distance) % size) for i in range(size)])


def swapped(array, axis):
    return lax.ppermute(array, axis, [(i, i ^ 1) for i in range(lax.axis_size(axis))])


def body(coupling, interior_solve, boundary_stiffness, migration):
    home, depth, width = interior_solve.shape
    blocks = width // LANES
    pieces = jnp.swapaxes(coupling, 1, 2)
    outgoing = pack(migration, pieces, interior_solve, True)
    arrived = [swapped(outgoing[0], "group"), swapped(outgoing[1], "group")]
    local = pack(migration, pieces, interior_solve, False)
    ups, downs, totals = [], [], [None, None]
    owns = []
    for slot in range(OWN):
        up, down, own = merge(migration, arrived[slot], local[slot], slot, home)
        ups.append(up)
        downs.append(down)
        owns.append(own)
    stiff_arrived = swapped(stiff_out(migration, boundary_stiffness), "group")
    stiff = stiff_merge(migration, boundary_stiffness, stiff_arrived)
    pending = [[(ups[slot], hops(slot)[0], owns[slot])] for slot in range(OWN)]
    for step in range(1, 4):
        for slot in range(OWN):
            sent_up = ups[slot] if step == 1 else ups[slot][1:]
            sent_down = downs[slot] if step == 1 else downs[slot][:-1]
            ups[slot] = shifted(sent_up, "tile_1", 1)
            downs[slot] = shifted(sent_down, "tile_1", -1)
        for slot in range(OWN):
            totals[slot] = accumulate(totals[slot], pending[slot], width, f"chunks_{slot}")
            left_up, left_down = hops(slot)[0] - step, hops(slot)[1] - step
            pending[slot] = [(ups[slot], left_up + 1, 0), (downs[slot], 0, blocks + left_down)]
    far = [shifted(ups[0][1:], "tile_1", 1), shifted(downs[1][:-1], "tile_1", -1)]
    keeps, others = [], []
    for slot in range(OWN):
        totals[slot] = accumulate(totals[slot], pending[slot], width, f"chunks_{slot}")
        first, index = (1, 0) if slot == 0 else (0, blocks)
        send, keep = last_chunk(totals[slot], far[slot], first, index, stiff, slot, f"last_{slot}")
        keeps.append(keep)
        others.append(swapped(send, "tile_0"))
    return finish(keeps, others)


def solution(mesh):
    finer = Mesh(mesh.devices.reshape(mesh.shape["group"], 2, 8), ("group", "tile_0", "tile_1"))
    in_specs = (P("group", None, TILE), P("group", TILE, None), P("group", TILE, None), P())
    out_specs = P("group", TILE, None)
    return jax.shard_map(body, mesh=finer, in_specs=in_specs, out_specs=out_specs, check_vma=False)
```

```python
import jax
import jax.numpy as jnp
from jax import lax
from jax.experimental import pallas as pl
from jax.experimental.pallas import tpu as pltpu
from jax.sharding import Mesh
from jax.sharding import PartitionSpec as P

OWN = 2
TILE = ("tile_0", "tile_1")
LANES = 128
PARAMS = pltpu.CompilerParams(vmem_limit_bytes=32 * 1024 * 1024)
SMEM = pl.BlockSpec(memory_space=pltpu.SMEM)
VMEM = pl.BlockSpec(memory_space=pltpu.VMEM)
HBM = pl.BlockSpec(memory_space=pltpu.HBM)


def hops(slot):
    return (3, 4) if slot == 0 else (4, 3)


def locate(plan, group, wanted, home):
    position, here = jnp.int32(0), jnp.bool_(False)
    for k in range(home):
        match = plan[group * home + k] == wanted
        position = jnp.where(match, jnp.int32(k), position)
        here = jnp.logical_or(here, match)
    return position, here


def pack(plan, coupling, solve, for_partner):
    home, depth, width = solve.shape
    blocks = width // LANES

    def kernel(plan_hbm, c_hbm, x_hbm, out0, out1, plan_ref, c_buf, x_buf, plan_sem, c_sem, x_sem):
        group = lax.axis_index("group")
        place = lax.axis_index("tile_1")
        owner = jnp.bitwise_xor(group, 1) if for_partner else group
        outs = (out0, out1)
        copies = [
            pltpu.make_async_copy(plan_hbm, plan_ref, plan_sem),
            pltpu.make_async_copy(c_hbm, c_buf, c_sem),
            pltpu.make_async_copy(x_hbm, x_buf, x_sem),
        ]
        for copy in copies:
            copy.start()
        low = lax.broadcasted_iota(jnp.int32, (depth, LANES), 1) < LANES // 2
        copies[0].wait()
        positions = [locate(plan_ref, group, owner * OWN + slot, home)[0] for slot in range(OWN)]
        copies[1].wait()
        for slot in range(OWN):
            up = hops(slot)[0]
            for m in range(blocks // 2):
                first = c_buf[positions[slot], :, pl.ds(m * LANES, LANES)]
                second = c_buf[positions[slot], :, pl.ds((m + blocks // 2) * LANES, LANES)]
                even = jnp.where(low, first, pltpu.roll(second, LANES // 2, 1))
                odd = jnp.where(low, pltpu.roll(first, LANES // 2, 1), second)
                for to, piece in ((2 * m, even), (2 * m + 1, odd)):
                    ahead = jnp.bitwise_and(to - place, blocks - 1)
                    spot = jnp.where(ahead == 0, 15, jnp.where(ahead <= up, ahead - 1, ahead + 7))
                    outs[slot][spot] = piece
        copies[2].wait()
        for slot in range(OWN):
            up = hops(slot)[0]
            for n in range(blocks):
                outs[slot][up + n] = x_buf[positions[slot], :, pl.ds(n * LANES, LANES)]

    packet = jax.ShapeDtypeStruct((2 * blocks, depth, LANES), jnp.float32)
    return pl.pallas_call(
        kernel,
        out_shape=(packet, packet),
        in_specs=[HBM] * 3,
        out_specs=(VMEM, VMEM),
        scratch_shapes=[
            pltpu.SMEM(plan.shape, jnp.int32),
            pltpu.VMEM((home, depth, width), jnp.float32),
            pltpu.VMEM((home, depth, width), jnp.float32),
            pltpu.SemaphoreType.DMA,
            pltpu.SemaphoreType.DMA,
            pltpu.SemaphoreType.DMA,
        ],
        compiler_params=PARAMS,
        name="pack_partner" if for_partner else "pack_own",
    )(plan, coupling, solve)


def merge(plan, arrived, local, slot, home):
    total, depth, _ = arrived.shape
    up, down = hops(slot)
    blocks = total // 2
    half = blocks // 2

    def kernel(plan_ref, arrived_ref, local_ref, up_ref, down_ref, own_ref):
        group = lax.axis_index("group")
        _, here = locate(plan_ref, group, group * OWN + slot, home)

        def put(source):
            up_ref[...] = source[0 : up + blocks]
            if slot == 0:
                down_ref[...] = source[up : total - 1]
            else:
                down_ref[0:half] = source[up + half : up + blocks]
                down_ref[half:blocks] = source[up : up + half]
                down_ref[blocks:] = source[up + blocks : total - 1]
            own_ref[...] = source[total - 1]

        @pl.when(here)
        def _():
            put(local_ref)

        @pl.when(jnp.logical_not(here))
        def _():
            put(arrived_ref)

    return pl.pallas_call(
        kernel,
        out_shape=(
            jax.ShapeDtypeStruct((up + blocks, depth, LANES), jnp.float32),
            jax.ShapeDtypeStruct((down + blocks, depth, LANES), jnp.float32),
            jax.ShapeDtypeStruct((depth, LANES), jnp.float32),
        ),
        in_specs=[SMEM, VMEM, VMEM],
        out_specs=(VMEM, VMEM, VMEM),
        compiler_params=PARAMS,
        name=f"merge_{slot}",
    )(plan, arrived, local)


def stiff_out(plan, stiff):
    home, rows, width = stiff.shape

    def kernel(plan_ref, b_hbm, out_ref, sem):
        group = lax.axis_index("group")
        copies = []
        for slot in range(OWN):
            position, _ = locate(plan_ref, group, jnp.bitwise_xor(group, 1) * OWN + slot, home)
            copy = pltpu.make_async_copy(b_hbm.at[position], out_ref.at[slot], sem.at[slot])
            copy.start()
            copies.append(copy)
        for copy in copies:
            copy.wait()

    return pl.pallas_call(
        kernel,
        out_shape=jax.ShapeDtypeStruct((OWN, rows, width), jnp.float32),
        in_specs=[SMEM, HBM],
        out_specs=VMEM,
        scratch_shapes=[pltpu.SemaphoreType.DMA((OWN,))],
        compiler_params=PARAMS,
        name="stiff_out",
    )(plan, stiff)


def stiff_merge(plan, stiff, arrived):
    home, rows, width = stiff.shape

    def kernel(plan_ref, b_hbm, arrived_ref, out_ref, sem):
        group = lax.axis_index("group")
        for slot in range(OWN):
            position, here = locate(plan_ref, group, group * OWN + slot, home)

            @pl.when(here)
            def _():
                copy = pltpu.make_async_copy(b_hbm.at[position], out_ref.at[slot], sem.at[slot])
                copy.start()
                copy.wait()

            @pl.when(jnp.logical_not(here))
            def _():
                out_ref[slot] = arrived_ref[slot]

    return pl.pallas_call(
        kernel,
        out_shape=jax.ShapeDtypeStruct((OWN, rows, width), jnp.float32),
        in_specs=[SMEM, HBM, VMEM],
        out_specs=VMEM,
        scratch_shapes=[pltpu.SemaphoreType.DMA((OWN,))],
        compiler_params=PARAMS,
        name="stiff_merge",
    )(plan, stiff, arrived)


def split(value):
    high = value.astype(jnp.bfloat16)
    return high, (value - high.astype(jnp.float32)).astype(jnp.bfloat16)


def add_chunks(total_ref, chunks, start):
    for packet, places, piece in chunks:
        c_high, c_low = split(piece)
        left = jnp.concatenate([c_high, c_high, c_low], axis=0)
        for n in range(0, len(places), 2):
            x = jnp.concatenate([packet[places[n]], packet[places[n + 1]]], axis=1)
            x_high, x_low = split(x)
            right = jnp.concatenate([x_high, x_low, x_high], axis=0)
            product = lax.dot_general(left, right, (((0,), (0,)), ((), ())), preferred_element_type=jnp.float32)
            where = (slice(None), pl.ds(n * LANES, 2 * LANES))
            total_ref[where] = product if start else total_ref[where] + product
        start = False


def gathered(sources):
    arrays, layout = [], []

    def place(array):
        for k, known in enumerate(arrays):
            if known is array:
                return k
        arrays.append(array)
        return len(arrays) - 1

    for packet, places, holder, index in sources:
        layout.append((place(packet), places, place(holder), index))
    return arrays, layout


def chunks_of(refs, layout):
    return [
        (refs[k], places, refs[holder][...] if index is None else refs[holder][index])
        for k, places, holder, index in layout
    ]


def accumulate(total, sources, width, name):
    arrays, layout = gathered(sources)
    given = [] if total is None else [total]
    n_given = len(given)

    def kernel(*refs):
        total_ref = refs[-1]
        if n_given:
            total_ref[...] = refs[0][...]
        add_chunks(total_ref, chunks_of(refs[n_given:-1], layout), not n_given)

    return pl.pallas_call(
        kernel,
        out_shape=jax.ShapeDtypeStruct((LANES, width), jnp.float32),
        in_specs=[VMEM] * (n_given + len(arrays)),
        out_specs=VMEM,
        input_output_aliases={0: 0} if n_given else {},
        compiler_params=PARAMS,
        cost_estimate=pl.CostEstimate(flops=2 * 144 * 128 * 1024, bytes_accessed=1 << 20, transcendentals=0),
        name=name,
    )(*given, *arrays)


def last_chunks(total, sources, stiff, slot, first, width, name):
    rows = LANES // 2
    arrays, layout = gathered(sources)
    columns = pl.ds(first, width)

    def kernel(total_ref, stiff_ref, *refs):
        send_ref, keep_ref, sum_ref = refs[-3:]
        sum_ref[...] = total_ref[:, columns]
        add_chunks(sum_ref, chunks_of(refs[:-3], layout), False)
        mine = lax.axis_index("tile_0")
        send_ref[...] = sum_ref[pl.ds(pl.multiple_of((1 - mine) * rows, rows), rows), :]
        keep_ref[...] = stiff_ref[slot, :, columns] - sum_ref[pl.ds(pl.multiple_of(mine * rows, rows), rows), :]

    half = jax.ShapeDtypeStruct((rows, width), jnp.float32)
    return pl.pallas_call(
        kernel,
        out_shape=(half, half),
        in_specs=[VMEM] * (2 + len(arrays)),
        out_specs=(VMEM, VMEM),
        scratch_shapes=[pltpu.VMEM((LANES, width), jnp.float32)],
        compiler_params=PARAMS,
        name=name,
    )(total, stiff, *arrays)


def finish(result, parts, slot, rows, width):
    flat = [array for pair in parts for array in pair]
    given = [] if result is None else [result]

    def kernel(*refs):
        ins = refs[len(given) : -3]
        out_hbm, buf, sem = refs[-3:]
        first = 0
        for k in range(0, len(ins), 2):
            columns = pl.ds(first, ins[k].shape[1])
            buf[:, columns] = ins[k][...] - ins[k + 1][...]
            first += ins[k].shape[1]
        copy = pltpu.make_async_copy(buf, out_hbm.at[slot], sem)
        copy.start()
        copy.wait()

    return pl.pallas_call(
        kernel,
        out_shape=jax.ShapeDtypeStruct((OWN, rows, width), jnp.float32),
        in_specs=[HBM] * len(given) + [VMEM] * len(flat),
        out_specs=HBM,
        scratch_shapes=[pltpu.VMEM((rows, width), jnp.float32), pltpu.SemaphoreType.DMA],
        input_output_aliases={0: 0} if given else {},
        compiler_params=PARAMS,
        name=f"finish_{slot}",
    )(*given, *flat)


def shifted(array, axis, distance):
    size = lax.axis_size(axis)
    return lax.ppermute(array, axis, [(i, (i + distance) % size) for i in range(size)])


def swapped(array, axis):
    return lax.ppermute(array, axis, [(i, i ^ 1) for i in range(lax.axis_size(axis))])


def up(array):
    return shifted(array, "tile_1", 1)


def down(array):
    return shifted(array, "tile_1", -1)


def body(coupling, interior_solve, boundary_stiffness, migration):
    home, depth, width = interior_solve.shape
    rows = boundary_stiffness.shape[1]
    blocks = width // LANES
    half = blocks // 2
    pieces = jnp.swapaxes(coupling, 1, 2)
    in_hbm = [pltpu.with_memory_space_constraint(a, pltpu.HBM) for a in (migration, pieces, interior_solve)]
    outgoing = pack(*in_hbm, True)
    arrived = [swapped(outgoing[0], "group"), swapped(outgoing[1], "group")]
    local = pack(*in_hbm, False)
    up0, down0, own0 = merge(migration, arrived[0], local[0], 0, home)
    up1, down1, own1 = merge(migration, arrived[1], local[1], 1, home)
    stiff_arrived = swapped(stiff_out(migration, boundary_stiffness), "group")
    stiff = stiff_merge(migration, boundary_stiffness, stiff_arrived)

    def run(first):
        return list(range(first, first + blocks))

    turned = list(range(half, blocks)) + list(range(half))
    u0, d0, u1, d1 = up(up0), down(down0), up(up1), down(down1)
    total0 = accumulate(None, [(up0, run(3), own0, None)], width, "chunks_0")
    total1 = accumulate(None, [(up1, run(4), own1, None)], width, "chunks_1")
    uu0, dd0 = up(u0[1:]), down(d0[:-1])
    total0 = accumulate(total0, [(u0, run(3), u0, 0), (d0, run(0), d0, blocks + 3)], width, "chunks_0")
    uu1, dd1 = up(u1[1:]), down(d1[:-1])
    total1 = accumulate(total1, [(u1, run(4), u1, 0), (d1, turned, d1, blocks + 2)], width, "chunks_1")
    uuu0, ddd0 = up(uu0[1:]), down(dd0[:-1])
    total0 = accumulate(total0, [(uu0, run(2), uu0, 0), (dd0, run(0), dd0, blocks + 2)], width, "chunks_0")
    uuu1a, ddd1a = up(uu1[1 : half + 3]), down(dd1[half : blocks + 1])
    total1 = accumulate(total1, [(uu1, run(3), uu1, 0), (dd1, turned, dd1, blocks + 1)], width, "chunks_1")
    far0a, far0b = up(uuu0[1 : half + 1]), down(ddd0[half : blocks + 1])
    total0 = accumulate(total0, [(uuu0, run(1), uuu0, 0), (ddd0, run(0), ddd0, blocks + 1)], width, "chunks_0")
    uuu1b, ddd1b = up(uu1[half + 3 :]), down(dd1[:half])
    far1a, far1b = up(uuu1a[1:]), down(ddd1b)
    left, right = list(range(half)), list(range(half, blocks))
    wide = width // 2
    send0a, keep0a = last_chunks(
        total0, [(far0a, left, far0b, half)], stiff, 0, 0, wide, "last_0a"
    )
    send0b, keep0b = last_chunks(
        total0, [(far0b, left, far0b, half)], stiff, 0, wide, wide, "last_0b"
    )
    del right
    other0a, other0b = swapped(send0a, "tile_0"), swapped(send0b, "tile_0")
    send1a, keep1a = last_chunks(
        total1,
        [(uuu1a, run(2)[:half], uuu1a, 0), (ddd1a, left, ddd1a, half), (far1a, run(1)[:half], far1a, 0)],
        stiff, 1, 0, wide, "last_1a",
    )
    other1a = swapped(send1a, "tile_0")
    send1b, keep1b = last_chunks(
        total1,
        [(uuu1b, left, uuu1a, 0), (ddd1b, left, ddd1a, half), (far1b, left, far1a, 0)],
        stiff, 1, wide, wide, "last_1b",
    )
    other1b = swapped(send1b, "tile_0")
    result = finish(None, [(keep0a, other0a), (keep0b, other0b)], 0, rows, width)
    return finish(result, [(keep1a, other1a), (keep1b, other1b)], 1, rows, width)


def solution(mesh):
    finer = Mesh(mesh.devices.reshape(mesh.shape["group"], 2, 8), ("group", "tile_0", "tile_1"))
    in_specs = (P("group", None, TILE), P("group", TILE, None), P("group", TILE, None), P())
    out_specs = P("group", TILE, None)
    return jax.shard_map(body, mesh=finer, in_specs=in_specs, out_specs=out_specs, check_vma=False)
```

```python
import jax
import jax.numpy as jnp
from jax import lax
from jax.experimental import pallas as pl
from jax.experimental.pallas import tpu as pltpu
from jax.sharding import Mesh
from jax.sharding import PartitionSpec as P

OWN = 2
TILE = ("tile_0", "tile_1")
LANES = 128
PARAMS = pltpu.CompilerParams(vmem_limit_bytes=32 * 1024 * 1024)
SMEM = pl.BlockSpec(memory_space=pltpu.SMEM)
VMEM = pl.BlockSpec(memory_space=pltpu.VMEM)
HBM = pl.BlockSpec(memory_space=pltpu.HBM)


def hops(chain):
    return (4, 3) if chain == 0 else (3, 4)


def slot_of(chain):
    column = lax.axis_index("tile_0")
    return column if chain == 0 else 1 - column


def locate(plan, group, wanted, home):
    position, here = jnp.int32(0), jnp.bool_(False)
    for k in range(home):
        match = plan[group * home + k] == wanted
        position = jnp.where(match, jnp.int32(k), position)
        here = jnp.logical_or(here, match)
    return position, here


def pack(plan, coupling, solve, for_partner):
    home, depth, width = solve.shape
    blocks = width // LANES

    def kernel(plan_hbm, c_hbm, x_hbm, out0, out1, plan_ref, c_buf, x_buf, plan_sem, c_sem, x_sem):
        group = lax.axis_index("group")
        place = lax.axis_index("tile_1")
        owner = jnp.bitwise_xor(group, 1) if for_partner else group
        outs = (out0, out1)
        copies = [
            pltpu.make_async_copy(plan_hbm, plan_ref, plan_sem),
            pltpu.make_async_copy(c_hbm, c_buf, c_sem),
            pltpu.make_async_copy(x_hbm, x_buf, x_sem),
        ]
        for copy in copies:
            copy.start()
        low = lax.broadcasted_iota(jnp.int32, (depth, LANES), 1) < LANES // 2
        copies[0].wait()
        positions = [locate(plan_ref, group, owner * OWN + slot_of(slot), home)[0] for slot in range(OWN)]
        copies[1].wait()
        for slot in range(OWN):
            up = hops(slot)[0]
            for m in range(blocks // 2):
                first = c_buf[positions[slot], :, pl.ds(m * LANES, LANES)]
                second = c_buf[positions[slot], :, pl.ds((m + blocks // 2) * LANES, LANES)]
                even = jnp.where(low, first, pltpu.roll(second, LANES // 2, 1))
                odd = jnp.where(low, pltpu.roll(first, LANES // 2, 1), second)
                for to, piece in ((2 * m, even), (2 * m + 1, odd)):
                    ahead = jnp.bitwise_and(to - place, blocks - 1)
                    spot = jnp.where(ahead == 0, 15, jnp.where(ahead <= up, ahead - 1, ahead + 7))
                    outs[slot][spot] = piece
        copies[2].wait()
        for slot in range(OWN):
            up = hops(slot)[0]
            for n in range(blocks):
                outs[slot][up + n] = x_buf[positions[slot], :, pl.ds(n * LANES, LANES)]

    packet = jax.ShapeDtypeStruct((2 * blocks, depth, LANES), jnp.float32)
    return pl.pallas_call(
        kernel,
        out_shape=(packet, packet),
        in_specs=[HBM] * 3,
        out_specs=(VMEM, VMEM),
        scratch_shapes=[
            pltpu.SMEM(plan.shape, jnp.int32),
            pltpu.VMEM((home, depth, width), jnp.float32),
            pltpu.VMEM((home, depth, width), jnp.float32),
            pltpu.SemaphoreType.DMA,
            pltpu.SemaphoreType.DMA,
            pltpu.SemaphoreType.DMA,
        ],
        compiler_params=PARAMS,
        name="pack_partner" if for_partner else "pack_own",
    )(plan, coupling, solve)


def merge(plan, arrived, local, chain, home):
    total, depth, _ = arrived.shape
    up, down = hops(chain)
    blocks = total // 2

    def kernel(plan_ref, arrived_ref, local_ref, up_ref, down_ref, own_ref):
        group = lax.axis_index("group")
        _, here = locate(plan_ref, group, group * OWN + slot_of(chain), home)

        def put(source):
            up_ref[...] = source[0 : up + blocks]
            down_ref[...] = source[up : total - 1]
            if chain == 0:
                own_ref[0] = source[total - 1]
            else:
                own_ref[0:blocks] = source[up : up + blocks]
                own_ref[blocks] = source[total - 1]

        @pl.when(here)
        def _():
            put(local_ref)

        @pl.when(jnp.logical_not(here))
        def _():
            put(arrived_ref)

    return pl.pallas_call(
        kernel,
        out_shape=(
            jax.ShapeDtypeStruct((up + blocks, depth, LANES), jnp.float32),
            jax.ShapeDtypeStruct((down + blocks, depth, LANES), jnp.float32),
            jax.ShapeDtypeStruct((1 if chain == 0 else 1 + blocks, depth, LANES), jnp.float32),
        ),
        in_specs=[SMEM, VMEM, VMEM],
        out_specs=(VMEM, VMEM, VMEM),
        compiler_params=PARAMS,
        name=f"merge_{chain}",
    )(plan, arrived, local)


def stiff_out(plan, stiff):
    home, rows, width = stiff.shape

    def kernel(plan_ref, b_hbm, out_ref, sem):
        group = lax.axis_index("group")
        copies = []
        for slot in range(OWN):
            position, _ = locate(plan_ref, group, jnp.bitwise_xor(group, 1) * OWN + slot, home)
            copy = pltpu.make_async_copy(b_hbm.at[position], out_ref.at[slot], sem.at[slot])
            copy.start()
            copies.append(copy)
        for copy in copies:
            copy.wait()

    return pl.pallas_call(
        kernel,
        out_shape=jax.ShapeDtypeStruct((OWN, rows, width), jnp.float32),
        in_specs=[SMEM, HBM],
        out_specs=VMEM,
        scratch_shapes=[pltpu.SemaphoreType.DMA((OWN,))],
        compiler_params=PARAMS,
        name="stiff_out",
    )(plan, stiff)


def stiff_merge(plan, stiff, arrived):
    home, rows, width = stiff.shape

    def kernel(plan_ref, b_hbm, arrived_ref, out_ref, sem):
        group = lax.axis_index("group")
        for slot in range(OWN):
            position, here = locate(plan_ref, group, group * OWN + slot, home)

            @pl.when(here)
            def _():
                copy = pltpu.make_async_copy(b_hbm.at[position], out_ref.at[slot], sem.at[slot])
                copy.start()
                copy.wait()

            @pl.when(jnp.logical_not(here))
            def _():
                out_ref[slot] = arrived_ref[slot]

    return pl.pallas_call(
        kernel,
        out_shape=jax.ShapeDtypeStruct((OWN, rows, width), jnp.float32),
        in_specs=[SMEM, HBM, VMEM],
        out_specs=VMEM,
        scratch_shapes=[pltpu.SemaphoreType.DMA((OWN,))],
        compiler_params=PARAMS,
        name="stiff_merge",
    )(plan, stiff, arrived)


def split(value):
    high = value.astype(jnp.bfloat16)
    return high, (value - high.astype(jnp.float32)).astype(jnp.bfloat16)


def add_chunks(total_ref, chunks, start):
    for packet, places, piece in chunks:
        c_high, c_low = split(piece)
        left = jnp.concatenate([c_high, c_high, c_low], axis=0)
        for n in range(0, len(places), 2):
            x = jnp.concatenate([packet[places[n]], packet[places[n + 1]]], axis=1)
            x_high, x_low = split(x)
            right = jnp.concatenate([x_high, x_low, x_high], axis=0)
            product = lax.dot_general(left, right, (((0,), (0,)), ((), ())), preferred_element_type=jnp.float32)
            where = (slice(None), pl.ds(n * LANES, 2 * LANES))
            total_ref[where] = product if start else total_ref[where] + product
        start = False


def gathered(sources):
    arrays, layout = [], []

    def place(array):
        for k, known in enumerate(arrays):
            if known is array:
                return k
        arrays.append(array)
        return len(arrays) - 1

    for packet, places, holder, index in sources:
        layout.append((place(packet), places, place(holder), index))
    return arrays, layout


def chunks_of(refs, layout):
    return [
        (refs[k], places, refs[holder][...] if index is None else refs[holder][index])
        for k, places, holder, index in layout
    ]


def accumulate(total, sources, width, name):
    arrays, layout = gathered(sources)
    given = [] if total is None else [total]
    n_given = len(given)

    def kernel(*refs):
        total_ref = refs[-1]
        if n_given:
            total_ref[...] = refs[0][...]
        add_chunks(total_ref, chunks_of(refs[n_given:-1], layout), not n_given)

    return pl.pallas_call(
        kernel,
        out_shape=jax.ShapeDtypeStruct((LANES, width), jnp.float32),
        in_specs=[VMEM] * (n_given + len(arrays)),
        out_specs=VMEM,
        input_output_aliases={0: 0} if n_given else {},
        compiler_params=PARAMS,
        cost_estimate=pl.CostEstimate(flops=2 * 144 * 128 * 1024, bytes_accessed=1 << 20, transcendentals=0),
        name=name,
    )(*given, *arrays)


def last_chunks(total, sources):
    rows, width = LANES // 2, total.shape[1]
    arrays, layout = gathered(sources)

    def kernel(total_ref, *refs):
        send_ref, keep_ref, sum_ref = refs[-3:]
        sum_ref[...] = total_ref[...]
        add_chunks(sum_ref, chunks_of(refs[:-3], layout), False)
        mine = lax.axis_index("tile_0")
        send_ref[...] = sum_ref[pl.ds(pl.multiple_of((1 - mine) * rows, rows), rows), :]
        keep_ref[...] = sum_ref[pl.ds(pl.multiple_of(mine * rows, rows), rows), :]

    half = jax.ShapeDtypeStruct((rows, width), jnp.float32)
    return pl.pallas_call(
        kernel,
        out_shape=(half, half),
        in_specs=[VMEM] * (1 + len(arrays)),
        out_specs=(VMEM, VMEM),
        scratch_shapes=[pltpu.VMEM((LANES, width), jnp.float32)],
        compiler_params=PARAMS,
        name="last_chunks",
    )(total, *arrays)


def finish(result, stiff, product, chain):
    rows, width = product.shape
    given = [] if result is None else [result]

    def kernel(*refs):
        stiff_ref, product_ref, out_hbm, buf, sem = refs[len(given) :]
        slot = slot_of(chain)
        buf[...] = stiff_ref[slot] - product_ref[...]
        copy = pltpu.make_async_copy(buf, out_hbm.at[slot], sem)
        copy.start()
        copy.wait()

    return pl.pallas_call(
        kernel,
        out_shape=jax.ShapeDtypeStruct((OWN, rows, width), jnp.float32),
        in_specs=[HBM] * len(given) + [VMEM, VMEM],
        out_specs=HBM,
        scratch_shapes=[pltpu.VMEM((rows, width), jnp.float32), pltpu.SemaphoreType.DMA],
        input_output_aliases={0: 0} if given else {},
        compiler_params=PARAMS,
        name=f"finish_{chain}",
    )(*given, stiff, product)


def shifted(array, axis, distance):
    size = lax.axis_size(axis)
    return lax.ppermute(array, axis, [(i, (i + distance) % size) for i in range(size)])


def swapped(array, axis):
    return lax.ppermute(array, axis, [(i, i ^ 1) for i in range(lax.axis_size(axis))])


def crossed(array, distance):
    size = lax.axis_size("tile_1")
    pairs = [(x * size + z, (1 - x) * size + (z + distance) % size) for x in range(2) for z in range(size)]
    return lax.ppermute(array, TILE, pairs)


def body(coupling, interior_solve, boundary_stiffness, migration):
    home, depth, width = interior_solve.shape
    blocks = width // LANES
    pieces = jnp.swapaxes(coupling, 1, 2)
    in_hbm = [pltpu.with_memory_space_constraint(a, pltpu.HBM) for a in (migration, pieces, interior_solve)]
    outgoing = pack(*in_hbm, True)
    arrived = [swapped(outgoing[0], "group"), swapped(outgoing[1], "group")]
    local = pack(*in_hbm, False)
    ups, downs, owns = [None, None], [None, None], [None, None]
    for chain in range(2):
        ups[chain], downs[chain], owns[chain] = merge(migration, arrived[chain], local[chain], chain, home)
    stiff_arrived = swapped(stiff_out(migration, boundary_stiffness), "group")
    stiff = stiff_merge(migration, boundary_stiffness, stiff_arrived)

    def run(first):
        return list(range(first, first + blocks))

    crossed_own = crossed(owns[1], 0)
    sources = [(ups[0], run(hops(0)[0]), owns[0], 0)]
    total = None
    for step in range(1, 4):
        for chain in range(2):
            if step == 1 and chain == 1:
                ups[chain], downs[chain] = crossed(ups[chain], 1), crossed(downs[chain], -1)
            else:
                sent_up = ups[chain] if step == 1 else ups[chain][1:]
                sent_down = downs[chain] if step == 1 else downs[chain][:-1]
                ups[chain], downs[chain] = shifted(sent_up, "tile_1", 1), shifted(sent_down, "tile_1", -1)
        total = accumulate(total, sources, width, f"chunks_{step}")
        sources = [] if step > 1 else [(crossed_own, run(0), crossed_own, blocks)]
        for chain in range(2):
            left_up, left_down = hops(chain)[0] - step, hops(chain)[1] - step
            sources.append((ups[chain], run(left_up + 1), ups[chain], 0))
            sources.append((downs[chain], run(0), downs[chain], blocks + left_down))
    far0, far1 = shifted(ups[0][1:], "tile_1", 1), shifted(downs[1][:-1], "tile_1", -1)
    total = accumulate(total, sources, width, "chunks_4")
    send, keep = last_chunks(total, [(far0, run(1), far0, 0), (far1, run(0), far1, blocks)])
    other = swapped(send, "tile_0")
    return finish(finish(None, stiff, keep, 0), stiff, other, 1)


def solution(mesh):
    finer = Mesh(mesh.devices.reshape(mesh.shape["group"], 2, 8), ("group", "tile_0", "tile_1"))
    in_specs = (P("group", None, TILE), P("group", TILE, None), P("group", TILE, None), P())
    out_specs = P("group", TILE, None)
    return jax.shard_map(body, mesh=finer, in_specs=in_specs, out_specs=out_specs, check_vma=False)
```

```python
import jax
import jax.numpy as jnp
from jax import lax
from jax.experimental import pallas as pl
from jax.experimental.pallas import tpu as pltpu
from jax.sharding import Mesh
from jax.sharding import PartitionSpec as P

OWN = 2
TILE = ("tile_0", "tile_1")
LANES = 128
PARAMS = pltpu.CompilerParams(vmem_limit_bytes=32 * 1024 * 1024)
SMEM = pl.BlockSpec(memory_space=pltpu.SMEM)
VMEM = pl.BlockSpec(memory_space=pltpu.VMEM)
HBM = pl.BlockSpec(memory_space=pltpu.HBM)


def hops(chain):
    return (4, 3) if chain == 0 else (3, 4)


def slot_of(chain):
    column = lax.axis_index("tile_0")
    return column if chain == 0 else 1 - column


def locate(plan, group, wanted, home):
    position, here = jnp.int32(0), jnp.bool_(False)
    for k in range(home):
        match = plan[group * home + k] == wanted
        position = jnp.where(match, jnp.int32(k), position)
        here = jnp.logical_or(here, match)
    return position, here


def pack(plan, coupling, solve, for_partner):
    home, depth, width = solve.shape
    blocks = width // LANES

    def kernel(plan_hbm, c_hbm, x_hbm, out0, out1, plan_ref, c_buf, x_buf, plan_sem, c_sem, x_sem):
        group = lax.axis_index("group")
        place = lax.axis_index("tile_1")
        owner = jnp.bitwise_xor(group, 1) if for_partner else group
        outs = (out0, out1)
        copies = [
            pltpu.make_async_copy(plan_hbm, plan_ref, plan_sem),
            pltpu.make_async_copy(c_hbm, c_buf, c_sem),
            pltpu.make_async_copy(x_hbm, x_buf, x_sem),
        ]
        for copy in copies:
            copy.start()
        low = lax.broadcasted_iota(jnp.int32, (depth, LANES), 1) < LANES // 2
        copies[0].wait()
        positions = [locate(plan_ref, group, owner * OWN + slot_of(slot), home)[0] for slot in range(OWN)]
        copies[1].wait()
        for slot in range(OWN):
            up = hops(slot)[0]
            for m in range(blocks // 2):
                first = c_buf[positions[slot], :, pl.ds(m * LANES, LANES)]
                second = c_buf[positions[slot], :, pl.ds((m + blocks // 2) * LANES, LANES)]
                even = jnp.where(low, first, pltpu.roll(second, LANES // 2, 1))
                odd = jnp.where(low, pltpu.roll(first, LANES // 2, 1), second)
                for to, piece in ((2 * m, even), (2 * m + 1, odd)):
                    ahead = jnp.bitwise_and(to - place, blocks - 1)
                    spot = jnp.where(ahead == 0, 15, jnp.where(ahead <= up, ahead - 1, ahead + 7))
                    outs[slot][spot] = piece
        copies[2].wait()
        for slot in range(OWN):
            up = hops(slot)[0]
            for n in range(blocks):
                outs[slot][up + n] = x_buf[positions[slot], :, pl.ds(n * LANES, LANES)]

    packet = jax.ShapeDtypeStruct((2 * blocks, depth, LANES), jnp.float32)
    return pl.pallas_call(
        kernel,
        out_shape=(packet, packet),
        in_specs=[HBM] * 3,
        out_specs=(VMEM, VMEM),
        scratch_shapes=[
            pltpu.SMEM(plan.shape, jnp.int32),
            pltpu.VMEM((home, depth, width), jnp.float32),
            pltpu.VMEM((home, depth, width), jnp.float32),
            pltpu.SemaphoreType.DMA,
            pltpu.SemaphoreType.DMA,
            pltpu.SemaphoreType.DMA,
        ],
        compiler_params=PARAMS,
        name="pack_partner" if for_partner else "pack_own",
    )(plan, coupling, solve)


def merge(plan, arrived, local, chain, home):
    total, depth, _ = arrived.shape
    up, down = hops(chain)
    blocks = total // 2

    def kernel(plan_ref, arrived_ref, local_ref, up_ref, down_ref, own_ref):
        group = lax.axis_index("group")
        _, here = locate(plan_ref, group, group * OWN + slot_of(chain), home)

        def put(source):
            up_ref[...] = source[0 : up + blocks]
            down_ref[...] = source[up : total - 1]
            if chain == 0:
                own_ref[0] = source[total - 1]
            else:
                own_ref[0:blocks] = source[up : up + blocks]
                own_ref[blocks] = source[total - 1]

        @pl.when(here)
        def _():
            put(local_ref)

        @pl.when(jnp.logical_not(here))
        def _():
            put(arrived_ref)

    return pl.pallas_call(
        kernel,
        out_shape=(
            jax.ShapeDtypeStruct((up + blocks, depth, LANES), jnp.float32),
            jax.ShapeDtypeStruct((down + blocks, depth, LANES), jnp.float32),
            jax.ShapeDtypeStruct((1 if chain == 0 else 1 + blocks, depth, LANES), jnp.float32),
        ),
        in_specs=[SMEM, VMEM, VMEM],
        out_specs=(VMEM, VMEM, VMEM),
        compiler_params=PARAMS,
        name=f"merge_{chain}",
    )(plan, arrived, local)


FIRST_ROWS = 16


def stiff_out(plan, stiff, part):
    home, rows, width = stiff.shape
    total = rows + FIRST_ROWS if part == 0 else rows - FIRST_ROWS

    def kernel(plan_ref, b_hbm, out_ref, sem):
        group = lax.axis_index("group")
        partner = jnp.bitwise_xor(group, 1)
        places = [locate(plan_ref, group, partner * OWN + slot, home)[0] for slot in range(OWN)]
        if part == 0:
            copies = [
                pltpu.make_async_copy(b_hbm.at[places[0]], out_ref.at[pl.ds(0, rows)], sem.at[0]),
                pltpu.make_async_copy(
                    b_hbm.at[places[1], pl.ds(0, FIRST_ROWS)], out_ref.at[pl.ds(rows, FIRST_ROWS)], sem.at[1]
                ),
            ]
        else:
            copies = [pltpu.make_async_copy(b_hbm.at[places[1], pl.ds(FIRST_ROWS, total)], out_ref, sem.at[0])]
        for copy in copies:
            copy.start()
        for copy in copies:
            copy.wait()

    return pl.pallas_call(
        kernel,
        out_shape=jax.ShapeDtypeStruct((total, width), jnp.float32),
        in_specs=[SMEM, HBM],
        out_specs=VMEM,
        scratch_shapes=[pltpu.SemaphoreType.DMA((2,))],
        compiler_params=PARAMS,
        name=f"stiff_out_{part}",
    )(plan, stiff)


def stiff_merge(plan, stiff, arrived):
    home, rows, width = stiff.shape

    def kernel(plan_ref, b_hbm, part0, part1, out_ref, sem):
        group = lax.axis_index("group")
        places = [locate(plan_ref, group, group * OWN + slot, home) for slot in range(OWN)]
        for slot in range(OWN):
            position, here = places[slot]

            @pl.when(here)
            def _():
                copy = pltpu.make_async_copy(b_hbm.at[position], out_ref.at[slot], sem.at[slot])
                copy.start()
                copy.wait()

            @pl.when(jnp.logical_not(here))
            def _():
                if slot == 0:
                    out_ref[0] = part0[0:rows]
                else:
                    out_ref[1, 0:FIRST_ROWS] = part0[rows:]
                    out_ref[1, FIRST_ROWS:] = part1[...]

    return pl.pallas_call(
        kernel,
        out_shape=jax.ShapeDtypeStruct((OWN, rows, width), jnp.float32),
        in_specs=[SMEM, HBM, VMEM, VMEM],
        out_specs=VMEM,
        scratch_shapes=[pltpu.SemaphoreType.DMA((OWN,))],
        compiler_params=PARAMS,
        name="stiff_merge",
    )(plan, stiff, *arrived)


def split(value):
    high = value.astype(jnp.bfloat16)
    return high, (value - high.astype(jnp.float32)).astype(jnp.bfloat16)


def add_chunks(total_ref, chunks, start):
    for packet, places, piece in chunks:
        c_high, c_low = split(piece)
        left = jnp.concatenate([c_high, c_high, c_low], axis=0)
        for n in range(0, len(places), 2):
            x = jnp.concatenate([packet[places[n]], packet[places[n + 1]]], axis=1)
            x_high, x_low = split(x)
            right = jnp.concatenate([x_high, x_low, x_high], axis=0)
            product = lax.dot_general(left, right, (((0,), (0,)), ((), ())), preferred_element_type=jnp.float32)
            where = (slice(None), pl.ds(n * LANES, 2 * LANES))
            total_ref[where] = product if start else total_ref[where] + product
        start = False


def gathered(sources):
    arrays, layout = [], []

    def place(array):
        for k, known in enumerate(arrays):
            if known is array:
                return k
        arrays.append(array)
        return len(arrays) - 1

    for packet, places, holder, index in sources:
        layout.append((place(packet), places, place(holder), index))
    return arrays, layout


def chunks_of(refs, layout):
    return [
        (refs[k], places, refs[holder][...] if index is None else refs[holder][index])
        for k, places, holder, index in layout
    ]


def accumulate(total, sources, width, name):
    arrays, layout = gathered(sources)
    given = [] if total is None else [total]
    n_given = len(given)

    def kernel(*refs):
        total_ref = refs[-1]
        if n_given:
            total_ref[...] = refs[0][...]
        add_chunks(total_ref, chunks_of(refs[n_given:-1], layout), not n_given)

    return pl.pallas_call(
        kernel,
        out_shape=jax.ShapeDtypeStruct((LANES, width), jnp.float32),
        in_specs=[VMEM] * (n_given + len(arrays)),
        out_specs=VMEM,
        input_output_aliases={0: 0} if n_given else {},
        compiler_params=PARAMS,
        cost_estimate=pl.CostEstimate(flops=2 * 144 * 128 * 1024, bytes_accessed=1 << 20, transcendentals=0),
        name=name,
    )(*given, *arrays)


def last_chunks(total, sources):
    rows, width = LANES // 2, total.shape[1]
    arrays, layout = gathered(sources)

    def kernel(total_ref, *refs):
        send_ref, keep_ref, sum_ref = refs[-3:]
        sum_ref[...] = total_ref[...]
        add_chunks(sum_ref, chunks_of(refs[:-3], layout), False)
        mine = lax.axis_index("tile_0")
        send_ref[...] = sum_ref[pl.ds(pl.multiple_of((1 - mine) * rows, rows), rows), :]
        keep_ref[...] = sum_ref[pl.ds(pl.multiple_of(mine * rows, rows), rows), :]

    half = jax.ShapeDtypeStruct((rows, width), jnp.float32)
    return pl.pallas_call(
        kernel,
        out_shape=(half, half),
        in_specs=[VMEM] * (1 + len(arrays)),
        out_specs=(VMEM, VMEM),
        scratch_shapes=[pltpu.VMEM((LANES, width), jnp.float32)],
        compiler_params=PARAMS,
        name="last_chunks",
    )(total, *arrays)


def finish(result, stiff, product, chain):
    rows, width = product.shape
    given = [] if result is None else [result]

    def kernel(*refs):
        stiff_ref, product_ref, out_hbm, buf, sem = refs[len(given) :]
        slot = slot_of(chain)
        buf[...] = stiff_ref[slot] - product_ref[...]
        copy = pltpu.make_async_copy(buf, out_hbm.at[slot], sem)
        copy.start()
        copy.wait()

    return pl.pallas_call(
        kernel,
        out_shape=jax.ShapeDtypeStruct((OWN, rows, width), jnp.float32),
        in_specs=[HBM] * len(given) + [VMEM, VMEM],
        out_specs=HBM,
        scratch_shapes=[pltpu.VMEM((rows, width), jnp.float32), pltpu.SemaphoreType.DMA],
        input_output_aliases={0: 0} if given else {},
        compiler_params=PARAMS,
        name=f"finish_{chain}",
    )(*given, stiff, product)


def shifted(array, axis, distance):
    size = lax.axis_size(axis)
    return lax.ppermute(array, axis, [(i, (i + distance) % size) for i in range(size)])


def swapped(array, axis):
    return lax.ppermute(array, axis, [(i, i ^ 1) for i in range(lax.axis_size(axis))])


def crossed(array, distance):
    size = lax.axis_size("tile_1")
    pairs = [(x * size + z, (1 - x) * size + (z + distance) % size) for x in range(2) for z in range(size)]
    return lax.ppermute(array, TILE, pairs)


def after(array, *earlier):
    return lax.optimization_barrier((array, *earlier))[0]


def body(coupling, interior_solve, boundary_stiffness, migration):
    home, depth, width = interior_solve.shape
    blocks = width // LANES
    pieces = jnp.swapaxes(coupling, 1, 2)
    in_hbm = [pltpu.with_memory_space_constraint(a, pltpu.HBM) for a in (migration, pieces, interior_solve)]
    outgoing = pack(*in_hbm, True)
    arrived = [swapped(outgoing[0], "group"), swapped(outgoing[1], "group")]
    local = pack(*in_hbm, False)
    up0, down0, own0 = merge(migration, arrived[0], local[0], 0, home)
    up1, down1, own1 = merge(migration, after(arrived[1], up0), local[1], 1, home)

    def run(first):
        return list(range(first, first + blocks))

    def onward(arrays, crossing):
        sent = [None] * 4
        for k in (3, 2, 1, 0):
            if arrays[k] is not None:
                distance = 1 if k % 2 == 0 else -1
                sent[k] = crossed(arrays[k], distance) if crossing and k > 1 else shifted(arrays[k], "tile_1", distance)
        return sent

    came = onward([up0, down0, up1, down1], True)
    stiff1 = swapped(stiff_out(migration, boundary_stiffness, 1), "group")
    total = accumulate(None, [(up0, run(hops(0)[0]), own0, 0)], width, "chunks_1")
    left = [hops(0)[0] - 1, hops(0)[1] - 1, hops(1)[0] - 1, hops(1)[1] - 1]
    for step in range(2, 5):
        sources, sent = [], []
        for k in range(4):
            upward = k % 2 == 0
            sources.append((came[k], run(left[k] + 1) if upward else run(0), came[k], 0 if upward else blocks + left[k]))
            sent.append((came[k][1:] if upward else came[k][:-1]) if left[k] else None)
            left[k] -= 1
        total = accumulate(total, sources, width, f"chunks_{step}")
        if step == 4:
            stiff0 = swapped(stiff_out(after(migration, came[1]), boundary_stiffness, 0), "group")
            crossed_own = crossed(after(own1, came[2], stiff1), 0)
        came = onward(sent, False)
    stiff = stiff_merge(migration, boundary_stiffness, (stiff0, stiff1))
    far0 = after(came[0], stiff0)
    total = accumulate(total, [(far0, run(1), far0, 0)], width, "chunks_5")
    send, keep = last_chunks(
        total, [(crossed_own, run(0), crossed_own, blocks), (came[3], run(0), came[3], blocks)]
    )
    other = swapped(send, "tile_0")
    return finish(finish(None, stiff, keep, 0), stiff, other, 1)


def solution(mesh):
    finer = Mesh(mesh.devices.reshape(mesh.shape["group"], 2, 8), ("group", "tile_0", "tile_1"))
    in_specs = (P("group", None, TILE), P("group", TILE, None), P("group", TILE, None), P())
    out_specs = P("group", TILE, None)
    return jax.shard_map(body, mesh=finer, in_specs=in_specs, out_specs=out_specs, check_vma=False)
```

```python
import jax
import jax.numpy as jnp
from jax import lax
from jax.experimental import pallas as pl
from jax.experimental.pallas import tpu as pltpu
from jax.sharding import Mesh
from jax.sharding import PartitionSpec as P

OWN = 2
TILE = ("tile_0", "tile_1")
LANES = 128
PARAMS = pltpu.CompilerParams(vmem_limit_bytes=32 * 1024 * 1024)
SMEM = pl.BlockSpec(memory_space=pltpu.SMEM)
VMEM = pl.BlockSpec(memory_space=pltpu.VMEM)
HBM = pl.BlockSpec(memory_space=pltpu.HBM)


def hops(slot):
    return (3, 4) if slot == 0 else (4, 3)


def locate(plan, group, wanted, home):
    position, here = jnp.int32(0), jnp.bool_(False)
    for k in range(home):
        match = plan[group * home + k] == wanted
        position = jnp.where(match, jnp.int32(k), position)
        here = jnp.logical_or(here, match)
    return position, here


def pack(plan, coupling, solve, for_partner):
    home, depth, width = solve.shape
    blocks = width // LANES

    def kernel(plan_given, c_hbm, x_hbm, out0, out1, plan_buf, c_buf, x_buf, plan_sem, c_sem, x_sem):
        group = lax.axis_index("group")
        place = lax.axis_index("tile_1")
        owner = jnp.bitwise_xor(group, 1) if for_partner else group
        outs = (out0, out1)
        copies = [
            pltpu.make_async_copy(c_hbm, c_buf, c_sem),
            pltpu.make_async_copy(x_hbm, x_buf, x_sem),
        ]
        for copy in copies:
            copy.start()
        plan_ref = plan_given
        if for_partner:
            plan_copy = pltpu.make_async_copy(plan_given, plan_buf, plan_sem)
            plan_copy.start()
            plan_ref = plan_buf
        low = lax.broadcasted_iota(jnp.int32, (depth, LANES), 1) < LANES // 2
        if for_partner:
            plan_copy.wait()
        positions = [locate(plan_ref, group, owner * OWN + slot, home)[0] for slot in range(OWN)]
        copies[0].wait()
        for slot in range(OWN):
            up = hops(slot)[0]
            for m in range(blocks // 2):
                first = c_buf[positions[slot], :, pl.ds(m * LANES, LANES)]
                second = c_buf[positions[slot], :, pl.ds((m + blocks // 2) * LANES, LANES)]
                even = jnp.where(low, first, pltpu.roll(second, LANES // 2, 1))
                odd = jnp.where(low, pltpu.roll(first, LANES // 2, 1), second)
                for to, piece in ((2 * m, even), (2 * m + 1, odd)):
                    ahead = jnp.bitwise_and(to - place, blocks - 1)
                    spot = jnp.where(ahead == 0, 15, jnp.where(ahead <= up, ahead - 1, ahead + 7))
                    outs[slot][spot] = piece
        copies[1].wait()
        for slot in range(OWN):
            up = hops(slot)[0]
            for n in range(blocks):
                outs[slot][up + n] = x_buf[positions[slot], :, pl.ds(n * LANES, LANES)]

    packet = jax.ShapeDtypeStruct((2 * blocks, depth, LANES), jnp.float32)
    return pl.pallas_call(
        kernel,
        out_shape=(packet, packet),
        in_specs=[HBM if for_partner else SMEM, HBM, HBM],
        out_specs=(VMEM, VMEM),
        scratch_shapes=[
            pltpu.SMEM(plan.shape, jnp.int32),
            pltpu.VMEM((home, depth, width), jnp.float32),
            pltpu.VMEM((home, depth, width), jnp.float32),
            pltpu.SemaphoreType.DMA,
            pltpu.SemaphoreType.DMA,
            pltpu.SemaphoreType.DMA,
        ],
        compiler_params=PARAMS,
        name="pack_partner" if for_partner else "pack_own",
    )(plan, coupling, solve)


def merge(plan, arrived, local, slot, home):
    total, depth, _ = arrived.shape
    up, down = hops(slot)
    blocks = total // 2
    half = blocks // 2

    def kernel(plan_ref, arrived_ref, local_ref, up_ref, down_ref, own_ref):
        group = lax.axis_index("group")
        _, here = locate(plan_ref, group, group * OWN + slot, home)

        def put(source):
            up_ref[...] = source[0 : up + blocks]
            if slot == 0:
                down_ref[...] = source[up : total - 1]
            else:
                down_ref[0:half] = source[up + half : up + blocks]
                down_ref[half:blocks] = source[up : up + half]
                down_ref[blocks:] = source[up + blocks : total - 1]
            own_ref[...] = source[total - 1]

        @pl.when(here)
        def _():
            put(local_ref)

        @pl.when(jnp.logical_not(here))
        def _():
            put(arrived_ref)

    return pl.pallas_call(
        kernel,
        out_shape=(
            jax.ShapeDtypeStruct((up + blocks, depth, LANES), jnp.float32),
            jax.ShapeDtypeStruct((down + blocks, depth, LANES), jnp.float32),
            jax.ShapeDtypeStruct((depth, LANES), jnp.float32),
        ),
        in_specs=[SMEM, VMEM, VMEM],
        out_specs=(VMEM, VMEM, VMEM),
        compiler_params=PARAMS,
        name=f"merge_{slot}",
    )(plan, arrived, local)


def stiff_out(plan, stiff):
    home, rows, width = stiff.shape

    def kernel(plan_ref, b_hbm, out_ref, sem):
        group = lax.axis_index("group")
        copies = []
        for slot in range(OWN):
            position, _ = locate(plan_ref, group, jnp.bitwise_xor(group, 1) * OWN + slot, home)
            copy = pltpu.make_async_copy(b_hbm.at[position], out_ref.at[slot], sem.at[slot])
            copy.start()
            copies.append(copy)
        for copy in copies:
            copy.wait()

    return pl.pallas_call(
        kernel,
        out_shape=jax.ShapeDtypeStruct((OWN, rows, width), jnp.float32),
        in_specs=[SMEM, HBM],
        out_specs=VMEM,
        scratch_shapes=[pltpu.SemaphoreType.DMA((OWN,))],
        compiler_params=PARAMS,
        name="stiff_out",
    )(plan, stiff)


def stiff_merge(plan, stiff, arrived):
    home, rows, width = stiff.shape

    def kernel(plan_ref, b_hbm, arrived_ref, out_ref, sem):
        group = lax.axis_index("group")
        for slot in range(OWN):
            position, here = locate(plan_ref, group, group * OWN + slot, home)

            @pl.when(here)
            def _():
                copy = pltpu.make_async_copy(b_hbm.at[position], out_ref.at[slot], sem.at[slot])
                copy.start()
                copy.wait()

            @pl.when(jnp.logical_not(here))
            def _():
                out_ref[slot] = arrived_ref[slot]

    return pl.pallas_call(
        kernel,
        out_shape=jax.ShapeDtypeStruct((OWN, rows, width), jnp.float32),
        in_specs=[SMEM, HBM, VMEM],
        out_specs=VMEM,
        scratch_shapes=[pltpu.SemaphoreType.DMA((OWN,))],
        compiler_params=PARAMS,
        name="stiff_merge",
    )(plan, stiff, arrived)


def split(value):
    high = value.astype(jnp.bfloat16)
    return high, (value - high.astype(jnp.float32)).astype(jnp.bfloat16)


def add_chunks(total_ref, chunks, start):
    for packets, places, piece in chunks:
        c_high, c_low = split(piece)
        left = jnp.concatenate([c_high, c_high, c_low], axis=0)
        each = len(places) // len(packets)
        for n in range(0, len(places), 2):
            packet = packets[n // each]
            x = jnp.concatenate([packet[places[n]], packet[places[n + 1]]], axis=1)
            x_high, x_low = split(x)
            right = jnp.concatenate([x_high, x_low, x_high], axis=0)
            product = lax.dot_general(left, right, (((0,), (0,)), ((), ())), preferred_element_type=jnp.float32)
            where = (slice(None), pl.ds(n * LANES, 2 * LANES))
            total_ref[where] = product if start else total_ref[where] + product
        start = False


def gathered(sources):
    arrays, layout = [], []

    def place(array):
        for k, known in enumerate(arrays):
            if known is array:
                return k
        arrays.append(array)
        return len(arrays) - 1

    for packets, places, holder, index in sources:
        packets = packets if isinstance(packets, tuple) else (packets,)
        layout.append((tuple(place(p) for p in packets), places, place(holder), index))
    return arrays, layout


def chunks_of(refs, layout):
    return [
        ([refs[k] for k in ks], places, refs[holder][...] if index is None else refs[holder][index])
        for ks, places, holder, index in layout
    ]


def accumulate(total, sources, width, name):
    arrays, layout = gathered(sources)
    given = [] if total is None else [total]
    n_given = len(given)

    def kernel(*refs):
        total_ref = refs[-1]
        if n_given:
            total_ref[...] = refs[0][...]
        add_chunks(total_ref, chunks_of(refs[n_given:-1], layout), not n_given)

    return pl.pallas_call(
        kernel,
        out_shape=jax.ShapeDtypeStruct((LANES, width), jnp.float32),
        in_specs=[VMEM] * (n_given + len(arrays)),
        out_specs=VMEM,
        input_output_aliases={0: 0} if n_given else {},
        compiler_params=PARAMS,
        cost_estimate=pl.CostEstimate(flops=2 * 144 * 128 * 1024, bytes_accessed=1 << 20, transcendentals=0),
        name=name,
    )(*given, *arrays)


def last_chunks(total, sources, first, width, name):
    rows = LANES // 2
    arrays, layout = gathered(sources)

    def kernel(total_ref, *refs):
        send_ref, keep_ref, sum_ref = refs[-3:]
        sum_ref[...] = total_ref[:, pl.ds(first, width)]
        add_chunks(sum_ref, chunks_of(refs[:-3], layout), False)
        mine = lax.axis_index("tile_0")
        send_ref[...] = sum_ref[pl.ds(pl.multiple_of((1 - mine) * rows, rows), rows), :]
        keep_ref[...] = sum_ref[pl.ds(pl.multiple_of(mine * rows, rows), rows), :]

    half = jax.ShapeDtypeStruct((rows, width), jnp.float32)
    return pl.pallas_call(
        kernel,
        out_shape=(half, half),
        in_specs=[VMEM] * (1 + len(arrays)),
        out_specs=(VMEM, VMEM),
        scratch_shapes=[pltpu.VMEM((LANES, width), jnp.float32)],
        compiler_params=PARAMS,
        name=name,
    )(total, *arrays)


def finish(result, stiff, parts, slot):
    flat = [array for pair in parts for array in pair]
    given = [] if result is None else [result]
    rows, width = stiff.shape[1:]

    def kernel(*refs):
        stiff_ref, *ins = refs[len(given) : -3]
        out_hbm, buf, sem = refs[-3:]
        first = 0
        for k in range(0, len(ins), 2):
            columns = pl.ds(first, ins[k].shape[1])
            buf[:, columns] = stiff_ref[slot, :, columns] - (ins[k][...] + ins[k + 1][...])
            first += ins[k].shape[1]
        copy = pltpu.make_async_copy(buf, out_hbm.at[slot], sem)
        copy.start()
        copy.wait()

    return pl.pallas_call(
        kernel,
        out_shape=jax.ShapeDtypeStruct((OWN, rows, width), jnp.float32),
        in_specs=[HBM] * len(given) + [VMEM] * (1 + len(flat)),
        out_specs=HBM,
        scratch_shapes=[pltpu.VMEM((rows, width), jnp.float32), pltpu.SemaphoreType.DMA],
        input_output_aliases={0: 0} if given else {},
        compiler_params=PARAMS,
        name=f"finish_{slot}",
    )(*given, stiff, *flat)


def shifted(array, axis, distance):
    size = lax.axis_size(axis)
    return lax.ppermute(array, axis, [(i, (i + distance) % size) for i in range(size)])


def swapped(array, axis):
    return lax.ppermute(array, axis, [(i, i ^ 1) for i in range(lax.axis_size(axis))])


def up(array):
    return shifted(array, "tile_1", 1)


def down(array):
    return shifted(array, "tile_1", -1)


def body(coupling, interior_solve, boundary_stiffness, migration):
    home, depth, width = interior_solve.shape
    rows = boundary_stiffness.shape[1]
    blocks = width // LANES
    half = blocks // 2
    pieces = jnp.swapaxes(coupling, 1, 2)
    in_hbm = [pltpu.with_memory_space_constraint(a, pltpu.HBM) for a in (migration, pieces, interior_solve)]
    outgoing = pack(*in_hbm, True)
    arrived = [swapped(outgoing[0], "group"), swapped(outgoing[1], "group")]
    local = pack(migration, *in_hbm[1:], False)
    up0, down0, own0 = merge(migration, arrived[0], local[0], 0, home)
    up1, down1, own1 = merge(migration, arrived[1], local[1], 1, home)
    stiff_arrived = swapped(stiff_out(migration, boundary_stiffness), "group")
    stiff = stiff_merge(migration, boundary_stiffness, stiff_arrived)

    def run(first):
        return list(range(first, first + blocks))

    turned = list(range(half, blocks)) + list(range(half))
    u0, d0, u1, d1 = up(up0), down(down0), up(up1), down(down1)
    total0 = accumulate(None, [(up0, run(3), own0, None)], width, "chunks_0")
    total1 = accumulate(None, [(up1, run(4), own1, None)], width, "chunks_1")
    uu0, dd0 = up(u0[1:]), down(d0[:-1])
    total0 = accumulate(total0, [(u0, run(3), u0, 0), (d0, run(0), d0, blocks + 3)], width, "chunks_0")
    uu1, dd1 = up(u1[1:]), down(d1[:-1])
    total1 = accumulate(total1, [(u1, run(4), u1, 0), (d1, turned, d1, blocks + 2)], width, "chunks_1")
    uuu0, ddd0 = up(uu0[1:]), down(dd0[:-1])
    total0 = accumulate(total0, [(uu0, run(2), uu0, 0), (dd0, run(0), dd0, blocks + 2)], width, "chunks_0")
    uuu1a, ddd1a = up(uu1[1 : half + 3]), down(dd1[half : blocks + 1])
    total1 = accumulate(total1, [(uu1, run(3), uu1, 0), (dd1, turned, dd1, blocks + 1)], width, "chunks_1")
    far0a, far0b = up(uuu0[1 : half + 1]), down(ddd0[half : blocks + 1])
    uuu1b, ddd1b = up(uu1[half + 3 :]), down(dd1[:half])
    far1a, far1b = up(uuu1a[1:]), down(ddd1b)
    left = list(range(half))
    wide = width // 2
    total0 = accumulate(total0, [(uuu0, run(1), uuu0, 0), (ddd0, run(0), ddd0, blocks + 1)], width, "chunks_0")
    send0, keep0 = last_chunks(
        total0, [((far0a, far0b), left + left, far0b, half)], 0, width, "last_0"
    )
    other0 = swapped(send0, "tile_0")
    send1a, keep1a = last_chunks(
        total1,
        [(uuu1a, run(2)[:half], uuu1a, 0), (ddd1a, left, ddd1a, half), (far1a, run(1)[:half], far1a, 0)],
        0, wide, "last_1a",
    )
    other1a = swapped(send1a, "tile_0")
    send1b, keep1b = last_chunks(
        total1,
        [(uuu1b, left, uuu1a, 0), (ddd1b, left, ddd1a, half), (far1b, left, far1a, 0)],
        wide, wide, "last_1b",
    )
    other1b = swapped(send1b, "tile_0")
    result = finish(None, stiff, [(keep0, other0)], 0)
    return finish(result, stiff, [(keep1a, other1a), (keep1b, other1b)], 1)


def solution(mesh):
    finer = Mesh(mesh.devices.reshape(mesh.shape["group"], 2, 8), ("group", "tile_0", "tile_1"))
    in_specs = (P("group", None, TILE), P("group", TILE, None), P("group", TILE, None), P())
    out_specs = P("group", TILE, None)
    return jax.shard_map(body, mesh=finer, in_specs=in_specs, out_specs=out_specs, check_vma=False)
```

```python
import jax
import jax.numpy as jnp
from jax import lax
from jax.experimental import pallas as pl
from jax.experimental.pallas import tpu as pltpu
from jax.sharding import Mesh
from jax.sharding import PartitionSpec as P

OWN = 2
TILE = ("tile_0", "tile_1")
LANES = 128
PARAMS = pltpu.CompilerParams(vmem_limit_bytes=32 * 1024 * 1024)
SMEM = pl.BlockSpec(memory_space=pltpu.SMEM)
VMEM = pl.BlockSpec(memory_space=pltpu.VMEM)
HBM = pl.BlockSpec(memory_space=pltpu.HBM)


def hops(slot):
    return (4, 3) if slot == 0 else (3, 4)


def locate(plan, group, wanted, home):
    position, here = jnp.int32(0), jnp.bool_(False)
    for k in range(home):
        match = plan[group * home + k] == wanted
        position = jnp.where(match, jnp.int32(k), position)
        here = jnp.logical_or(here, match)
    return position, here


def pack(plan, coupling, solve, for_partner):
    home, depth, width = solve.shape
    blocks = width // LANES

    def kernel(plan_given, c_hbm, x_hbm, out0, out1, plan_buf, c_buf, x_buf, plan_sem, c_sem, x_sem):
        group = lax.axis_index("group")
        place = lax.axis_index("tile_1")
        owner = jnp.bitwise_xor(group, 1) if for_partner else group
        outs = (out0, out1)
        copies = [
            pltpu.make_async_copy(c_hbm, c_buf, c_sem),
            pltpu.make_async_copy(x_hbm, x_buf, x_sem),
        ]
        for copy in copies:
            copy.start()
        plan_ref = plan_given
        if for_partner:
            plan_copy = pltpu.make_async_copy(plan_given, plan_buf, plan_sem)
            plan_copy.start()
            plan_ref = plan_buf
        low = lax.broadcasted_iota(jnp.int32, (depth, LANES), 1) < LANES // 2
        if for_partner:
            plan_copy.wait()
        positions = [locate(plan_ref, group, owner * OWN + slot, home)[0] for slot in range(OWN)]
        copies[0].wait()
        for slot in range(OWN):
            up = hops(slot)[0]
            for m in range(blocks // 2):
                first = c_buf[positions[slot], :, pl.ds(m * LANES, LANES)]
                second = c_buf[positions[slot], :, pl.ds((m + blocks // 2) * LANES, LANES)]
                even = jnp.where(low, first, pltpu.roll(second, LANES // 2, 1))
                odd = jnp.where(low, pltpu.roll(first, LANES // 2, 1), second)
                for to, piece in ((2 * m, even), (2 * m + 1, odd)):
                    ahead = jnp.bitwise_and(to - place, blocks - 1)
                    spot = jnp.where(ahead == 0, 15, jnp.where(ahead <= up, ahead - 1, ahead + 7))
                    outs[slot][spot] = piece
        copies[1].wait()
        for slot in range(OWN):
            up = hops(slot)[0]
            for n in range(blocks):
                outs[slot][up + n] = x_buf[positions[slot], :, pl.ds(n * LANES, LANES)]

    packet = jax.ShapeDtypeStruct((2 * blocks, depth, LANES), jnp.float32)
    return pl.pallas_call(
        kernel,
        out_shape=(packet, packet),
        in_specs=[HBM if for_partner else SMEM, HBM, HBM],
        out_specs=(VMEM, VMEM),
        scratch_shapes=[
            pltpu.SMEM(plan.shape, jnp.int32),
            pltpu.VMEM((home, depth, width), jnp.float32),
            pltpu.VMEM((home, depth, width), jnp.float32),
            pltpu.SemaphoreType.DMA,
            pltpu.SemaphoreType.DMA,
            pltpu.SemaphoreType.DMA,
        ],
        compiler_params=PARAMS,
        name="pack_partner" if for_partner else "pack_own",
    )(plan, coupling, solve)


def merge(plan, arrived, local, slot, home):
    total, depth, _ = arrived.shape
    up, down = hops(slot)
    blocks = total // 2

    def kernel(plan_ref, arrived_ref, local_ref, up_ref, down_ref, own_ref):
        group = lax.axis_index("group")
        _, here = locate(plan_ref, group, group * OWN + slot, home)

        def put(source):
            up_ref[...] = source[0 : up + blocks]
            down_ref[...] = source[up : total - 1]
            own_ref[...] = source[total - 1]

        @pl.when(here)
        def _():
            put(local_ref)

        @pl.when(jnp.logical_not(here))
        def _():
            put(arrived_ref)

    return pl.pallas_call(
        kernel,
        out_shape=(
            jax.ShapeDtypeStruct((up + blocks, depth, LANES), jnp.float32),
            jax.ShapeDtypeStruct((down + blocks, depth, LANES), jnp.float32),
            jax.ShapeDtypeStruct((depth, LANES), jnp.float32),
        ),
        in_specs=[SMEM, VMEM, VMEM],
        out_specs=(VMEM, VMEM, VMEM),
        compiler_params=PARAMS,
        name=f"merge_{slot}",
    )(plan, arrived, local)


def stiff_out(plan, stiff):
    home, rows, width = stiff.shape

    def kernel(plan_ref, b_hbm, out_ref, sem):
        group = lax.axis_index("group")
        copies = []
        for slot in range(OWN):
            position, _ = locate(plan_ref, group, jnp.bitwise_xor(group, 1) * OWN + slot, home)
            copy = pltpu.make_async_copy(b_hbm.at[position], out_ref.at[slot], sem.at[slot])
            copy.start()
            copies.append(copy)
        for copy in copies:
            copy.wait()

    return pl.pallas_call(
        kernel,
        out_shape=jax.ShapeDtypeStruct((OWN, rows, width), jnp.float32),
        in_specs=[SMEM, HBM],
        out_specs=VMEM,
        scratch_shapes=[pltpu.SemaphoreType.DMA((OWN,))],
        compiler_params=PARAMS,
        name="stiff_out",
    )(plan, stiff)


def stiff_merge(plan, stiff, arrived):
    home, rows, width = stiff.shape

    def kernel(plan_ref, b_hbm, arrived_ref, out_ref, sem):
        group = lax.axis_index("group")
        for slot in range(OWN):
            position, here = locate(plan_ref, group, group * OWN + slot, home)

            @pl.when(here)
            def _():
                copy = pltpu.make_async_copy(b_hbm.at[position], out_ref.at[slot], sem.at[slot])
                copy.start()
                copy.wait()

            @pl.when(jnp.logical_not(here))
            def _():
                out_ref[slot] = arrived_ref[slot]

    return pl.pallas_call(
        kernel,
        out_shape=jax.ShapeDtypeStruct((OWN, rows, width), jnp.float32),
        in_specs=[SMEM, HBM, VMEM],
        out_specs=VMEM,
        scratch_shapes=[pltpu.SemaphoreType.DMA((OWN,))],
        compiler_params=PARAMS,
        name="stiff_merge",
    )(plan, stiff, arrived)


def split(value):
    high = value.astype(jnp.bfloat16)
    return high, (value - high.astype(jnp.float32)).astype(jnp.bfloat16)


def add_chunks(total_ref, chunks, start):
    for packets, places, piece in chunks:
        c_high, c_low = split(piece)
        left = jnp.concatenate([c_high, c_high, c_low], axis=0)
        each = len(places) // len(packets)
        for n in range(0, len(places), 2):
            packet = packets[n // each]
            x = jnp.concatenate([packet[places[n]], packet[places[n + 1]]], axis=1)
            x_high, x_low = split(x)
            right = jnp.concatenate([x_high, x_low, x_high], axis=0)
            product = lax.dot_general(left, right, (((0,), (0,)), ((), ())), preferred_element_type=jnp.float32)
            where = (slice(None), pl.ds(n * LANES, 2 * LANES))
            total_ref[where] = product if start else total_ref[where] + product
        start = False


def gathered(sources):
    arrays, layout = [], []

    def place(array):
        for k, known in enumerate(arrays):
            if known is array:
                return k
        arrays.append(array)
        return len(arrays) - 1

    for packets, places, holder, index in sources:
        packets = packets if isinstance(packets, tuple) else (packets,)
        layout.append((tuple(place(p) for p in packets), places, place(holder), index))
    return arrays, layout


def chunks_of(refs, layout):
    return [
        ([refs[k] for k in ks], places, refs[holder][...] if index is None else refs[holder][index])
        for ks, places, holder, index in layout
    ]


def accumulate(total, sources, width, name):
    arrays, layout = gathered(sources)
    given = [] if total is None else [total]
    n_given = len(given)

    def kernel(*refs):
        total_ref = refs[-1]
        if n_given:
            total_ref[...] = refs[0][...]
        add_chunks(total_ref, chunks_of(refs[n_given:-1], layout), not n_given)

    return pl.pallas_call(
        kernel,
        out_shape=jax.ShapeDtypeStruct((LANES, width), jnp.float32),
        in_specs=[VMEM] * (n_given + len(arrays)),
        out_specs=VMEM,
        compiler_params=PARAMS,
        cost_estimate=pl.CostEstimate(flops=2 * 144 * 128 * 1024, bytes_accessed=1 << 20, transcendentals=0),
        name=name,
    )(*given, *arrays)


def last_chunks(total, sources, first, width, name):
    rows = LANES // 2
    arrays, layout = gathered(sources)

    def kernel(total_ref, *refs):
        send_ref, keep_ref, sum_ref = refs[-3:]
        sum_ref[...] = total_ref[:, pl.ds(first, width)]
        add_chunks(sum_ref, chunks_of(refs[:-3], layout), False)
        mine = lax.axis_index("tile_0")
        send_ref[...] = sum_ref[pl.ds(pl.multiple_of((1 - mine) * rows, rows), rows), :]
        keep_ref[...] = sum_ref[pl.ds(pl.multiple_of(mine * rows, rows), rows), :]

    half = jax.ShapeDtypeStruct((rows, width), jnp.float32)
    return pl.pallas_call(
        kernel,
        out_shape=(half, half),
        in_specs=[VMEM] * (1 + len(arrays)),
        out_specs=(VMEM, VMEM),
        scratch_shapes=[pltpu.VMEM((LANES, width), jnp.float32)],
        compiler_params=PARAMS,
        name=name,
    )(total, *arrays)


def finish(result, stiff, parts, slot):
    flat = [array for pair in parts for array in pair]
    given = [] if result is None else [result]
    rows, width = stiff.shape[1:]

    def kernel(*refs):
        stiff_ref, *ins = refs[len(given) : -3]
        out_hbm, buf, sem = refs[-3:]
        first = 0
        for k in range(0, len(ins), 2):
            columns = pl.ds(first, ins[k].shape[1])
            buf[:, columns] = stiff_ref[slot, :, columns] - (ins[k][...] + ins[k + 1][...])
            first += ins[k].shape[1]
        copy = pltpu.make_async_copy(buf, out_hbm.at[slot], sem)
        copy.start()
        copy.wait()

    return pl.pallas_call(
        kernel,
        out_shape=jax.ShapeDtypeStruct((OWN, rows, width), jnp.float32),
        in_specs=[HBM] * len(given) + [VMEM] * (1 + len(flat)),
        out_specs=HBM,
        scratch_shapes=[pltpu.VMEM((rows, width), jnp.float32), pltpu.SemaphoreType.DMA],
        input_output_aliases={0: 0} if given else {},
        compiler_params=PARAMS,
        name=f"finish_{slot}",
    )(*given, stiff, *flat)


def shifted(array, axis, distance):
    size = lax.axis_size(axis)
    return lax.ppermute(array, axis, [(i, (i + distance) % size) for i in range(size)])


def swapped(array, axis):
    return lax.ppermute(array, axis, [(i, i ^ 1) for i in range(lax.axis_size(axis))])


def after(array, *earlier):
    return lax.optimization_barrier((array, *earlier))[0]


def up(array):
    return shifted(array, "tile_1", 1)


def down(array):
    return shifted(array, "tile_1", -1)


def body(coupling, interior_solve, boundary_stiffness, migration):
    home, depth, width = interior_solve.shape
    rows = boundary_stiffness.shape[1]
    blocks = width // LANES
    half = blocks // 2
    pieces = jnp.swapaxes(coupling, 1, 2)
    in_hbm = [pltpu.with_memory_space_constraint(a, pltpu.HBM) for a in (migration, pieces, interior_solve)]
    outgoing = pack(*in_hbm, True)
    arrived = [swapped(outgoing[0], "group"), swapped(outgoing[1], "group")]
    local = pack(migration, *in_hbm[1:], False)
    up0, down0, own0 = merge(migration, arrived[0], local[0], 0, home)
    up1, down1, own1 = merge(migration, arrived[1], local[1], 1, home)
    stiff_arrived = swapped(stiff_out(migration, boundary_stiffness), "group")
    stiff = stiff_merge(migration, boundary_stiffness, stiff_arrived)

    def run(first):
        return list(range(first, first + blocks))

    left = list(range(half))
    u0, d0, u1, d1 = up(up0), down(down0), up(up1), down(down1)
    uu0, dd0 = up(u0[1:]), down(d0[:-1])
    uu1, dd1 = up(u1[1:]), down(d1[:-1])
    total0 = accumulate(
        None, [(up0, run(4), own0, None), (u0, run(4), u0, 0), (d0, run(0), d0, blocks + 2)], width, "chunks_0"
    )
    uuu0, ddd0 = up(uu0[1:]), down(dd0[:-1])
    total1 = accumulate(
        None, [(up1, run(3), own1, None), (u1, run(3), u1, 0), (d1, run(0), d1, blocks + 3)], width, "chunks_1"
    )
    uuu1a, ddd1b = up(after(uu1[1 : half + 2], total0)), down(dd1[half : blocks + 2])
    ready0 = accumulate(total0, [(uu0, run(3), uu0, 0), (dd0, run(0), dd0, blocks + 1)], width, "chunks_0")
    far0a, far0b = up(after(uuu0[1 : half + 2], total1)), down(ddd0[half:blocks])
    far1a, far1b = up(uuu1a[1:]), down(after(ddd1b[: half + 1], ready0))
    ready1 = accumulate(total1, [(uu1, run(2), uu1, 0), (dd1, run(0), dd1, blocks + 2)], width, "chunks_1")
    uuu1b, ddd1a = up(after(uu1[half + 2 :], ready1)), down(dd1[:half])
    send0, keep0 = last_chunks(
        ready0,
        [
            (uuu0, run(2), uuu0, 0),
            (ddd0, run(0), ddd0, blocks),
            ((far0a, far0b), [1, 2, 3, 4, 0, 1, 2, 3], far0a, 0),
        ],
        0, width, "last_0",
    )
    other0 = swapped(send0, "tile_0")
    send1, keep1 = last_chunks(
        ready1,
        [
            ((uuu1a, uuu1b), [1, 2, 3, 4, 0, 1, 2, 3], uuu1a, 0),
            ((ddd1a, ddd1b), left + left, ddd1b, half + 1),
            ((far1a, far1b), left + left, far1b, half),
        ],
        0, width, "last_1",
    )
    other1 = swapped(send1, "tile_0")
    result = finish(None, stiff, [(keep0, other0)], 0)
    return finish(result, stiff, [(keep1, other1)], 1)


def solution(mesh):
    finer = Mesh(mesh.devices.reshape(mesh.shape["group"], 2, 8), ("group", "tile_0", "tile_1"))
    in_specs = (P("group", None, TILE), P("group", TILE, None), P("group", TILE, None), P())
    out_specs = P("group", TILE, None)
    return jax.shard_map(body, mesh=finer, in_specs=in_specs, out_specs=out_specs, check_vma=False)
```

```python
import jax
import jax.numpy as jnp
from jax import lax
from jax.experimental import pallas as pl
from jax.experimental.pallas import tpu as pltpu
from jax.sharding import Mesh
from jax.sharding import PartitionSpec as P

OWN = 2
TILE = ("tile_0", "tile_1")
LANES = 128
PARAMS = pltpu.CompilerParams(vmem_limit_bytes=32 * 1024 * 1024)
SMEM = pl.BlockSpec(memory_space=pltpu.SMEM)
VMEM = pl.BlockSpec(memory_space=pltpu.VMEM)
HBM = pl.BlockSpec(memory_space=pltpu.HBM)


def hops(chain):
    return (4, 3) if chain == 0 else (3, 4)


def slot_of(chain):
    column = lax.axis_index("tile_0")
    return column if chain == 0 else 1 - column


def locate(plan, group, wanted, home):
    position, here = jnp.int32(0), jnp.bool_(False)
    for k in range(home):
        match = plan[group * home + k] == wanted
        position = jnp.where(match, jnp.int32(k), position)
        here = jnp.logical_or(here, match)
    return position, here


def pack(plan, coupling, solve, for_partner):
    home, depth, width = solve.shape
    blocks = width // LANES

    def kernel(plan_given, c_hbm, x_hbm, out0, out1, plan_buf, c_buf, x_buf, plan_sem, c_sem, x_sem):
        group = lax.axis_index("group")
        place = lax.axis_index("tile_1")
        owner = jnp.bitwise_xor(group, 1) if for_partner else group
        outs = (out0, out1)
        copies = [
            pltpu.make_async_copy(c_hbm, c_buf, c_sem),
            pltpu.make_async_copy(x_hbm, x_buf, x_sem),
        ]
        for copy in copies:
            copy.start()
        plan_ref = plan_given
        if for_partner:
            plan_copy = pltpu.make_async_copy(plan_given, plan_buf, plan_sem)
            plan_copy.start()
            plan_ref = plan_buf
        low = lax.broadcasted_iota(jnp.int32, (depth, LANES), 1) < LANES // 2
        if for_partner:
            plan_copy.wait()
        positions = [locate(plan_ref, group, owner * OWN + slot_of(slot), home)[0] for slot in range(OWN)]
        copies[0].wait()
        for slot in range(OWN):
            up = hops(slot)[0]
            for m in range(blocks // 2):
                first = c_buf[positions[slot], :, pl.ds(m * LANES, LANES)]
                second = c_buf[positions[slot], :, pl.ds((m + blocks // 2) * LANES, LANES)]
                even = jnp.where(low, first, pltpu.roll(second, LANES // 2, 1))
                odd = jnp.where(low, pltpu.roll(first, LANES // 2, 1), second)
                for to, piece in ((2 * m, even), (2 * m + 1, odd)):
                    ahead = jnp.bitwise_and(to - place, blocks - 1)
                    spot = jnp.where(ahead == 0, 15, jnp.where(ahead <= up, ahead - 1, ahead + 7))
                    outs[slot][spot] = piece
        copies[1].wait()
        for slot in range(OWN):
            up = hops(slot)[0]
            for n in range(blocks):
                outs[slot][up + n] = x_buf[positions[slot], :, pl.ds(n * LANES, LANES)]

    packet = jax.ShapeDtypeStruct((2 * blocks, depth, LANES), jnp.float32)
    return pl.pallas_call(
        kernel,
        out_shape=(packet, packet),
        in_specs=[HBM if for_partner else SMEM, HBM, HBM],
        out_specs=(VMEM, VMEM),
        scratch_shapes=[
            pltpu.SMEM(plan.shape, jnp.int32),
            pltpu.VMEM((home, depth, width), jnp.float32),
            pltpu.VMEM((home, depth, width), jnp.float32),
            pltpu.SemaphoreType.DMA,
            pltpu.SemaphoreType.DMA,
            pltpu.SemaphoreType.DMA,
        ],
        compiler_params=PARAMS,
        name="pack_partner" if for_partner else "pack_own",
    )(plan, coupling, solve)


def merge(plan, arrived, local, chain, home):
    def kernel(plan_ref, arrived_ref, local_ref, out_ref):
        group = lax.axis_index("group")
        _, here = locate(plan_ref, group, group * OWN + slot_of(chain), home)

        @pl.when(here)
        def _():
            out_ref[...] = local_ref[...]

        @pl.when(jnp.logical_not(here))
        def _():
            out_ref[...] = arrived_ref[...]

    return pl.pallas_call(
        kernel,
        out_shape=jax.ShapeDtypeStruct(arrived.shape, jnp.float32),
        in_specs=[SMEM, VMEM, VMEM],
        out_specs=VMEM,
        compiler_params=PARAMS,
        name=f"merge_{chain}",
    )(plan, arrived, local)


def stiff_out(plan, stiff):
    home, rows, width = stiff.shape

    def kernel(plan_ref, b_hbm, out_ref, sem):
        group = lax.axis_index("group")
        copies = []
        for slot in range(OWN):
            position, _ = locate(plan_ref, group, jnp.bitwise_xor(group, 1) * OWN + slot, home)
            copy = pltpu.make_async_copy(b_hbm.at[position], out_ref.at[slot], sem.at[slot])
            copy.start()
            copies.append(copy)
        for copy in copies:
            copy.wait()

    return pl.pallas_call(
        kernel,
        out_shape=jax.ShapeDtypeStruct((OWN, rows, width), jnp.float32),
        in_specs=[SMEM, HBM],
        out_specs=VMEM,
        scratch_shapes=[pltpu.SemaphoreType.DMA((OWN,))],
        compiler_params=PARAMS,
        name="stiff_out",
    )(plan, stiff)


def stiff_merge(plan, stiff, arrived):
    home, rows, width = stiff.shape

    def kernel(plan_ref, b_hbm, arrived_ref, out_ref, sem):
        group = lax.axis_index("group")
        for slot in range(OWN):
            position, here = locate(plan_ref, group, group * OWN + slot, home)

            @pl.when(here)
            def _():
                copy = pltpu.make_async_copy(b_hbm.at[position], out_ref.at[slot], sem.at[slot])
                copy.start()
                copy.wait()

            @pl.when(jnp.logical_not(here))
            def _():
                out_ref[slot] = arrived_ref[slot]

    return pl.pallas_call(
        kernel,
        out_shape=jax.ShapeDtypeStruct((OWN, rows, width), jnp.float32),
        in_specs=[SMEM, HBM, VMEM],
        out_specs=VMEM,
        scratch_shapes=[pltpu.SemaphoreType.DMA((OWN,))],
        compiler_params=PARAMS,
        name="stiff_merge",
    )(plan, stiff, arrived)


def split(value):
    high = value.astype(jnp.bfloat16)
    return high, (value - high.astype(jnp.float32)).astype(jnp.bfloat16)


def add_chunks(total_ref, chunks, start):
    for packets, places, piece in chunks:
        c_high, c_low = split(piece)
        left = jnp.concatenate([c_high, c_high, c_low], axis=0)
        each = len(places) // len(packets)
        for n in range(0, len(places), 2):
            packet = packets[n // each]
            x = jnp.concatenate([packet[places[n]], packet[places[n + 1]]], axis=1)
            x_high, x_low = split(x)
            right = jnp.concatenate([x_high, x_low, x_high], axis=0)
            product = lax.dot_general(left, right, (((0,), (0,)), ((), ())), preferred_element_type=jnp.float32)
            where = (slice(None), pl.ds(n * LANES, 2 * LANES))
            total_ref[where] = product if start else total_ref[where] + product
        start = False


def gathered(sources):
    arrays, layout = [], []

    def place(array):
        for k, known in enumerate(arrays):
            if known is array:
                return k
        arrays.append(array)
        return len(arrays) - 1

    for packets, places, holder, index in sources:
        packets = packets if isinstance(packets, tuple) else (packets,)
        layout.append((tuple(place(p) for p in packets), places, place(holder), index))
    return arrays, layout


def chunks_of(refs, layout):
    return [
        ([refs[k] for k in ks], places, refs[holder][...] if index is None else refs[holder][index])
        for ks, places, holder, index in layout
    ]


def accumulate(total, sources, width, name):
    arrays, layout = gathered(sources)
    given = [] if total is None else [total]
    n_given = len(given)

    def kernel(*refs):
        total_ref = refs[-1]
        if n_given:
            total_ref[...] = refs[0][...]
        add_chunks(total_ref, chunks_of(refs[n_given:-1], layout), not n_given)

    return pl.pallas_call(
        kernel,
        out_shape=jax.ShapeDtypeStruct((LANES, width), jnp.float32),
        in_specs=[VMEM] * (n_given + len(arrays)),
        out_specs=VMEM,
        compiler_params=PARAMS,
        cost_estimate=pl.CostEstimate(flops=2 * 144 * 128 * 1024, bytes_accessed=1 << 20, transcendentals=0),
        name=name,
    )(*given, *arrays)


def last_chunks(total, sources):
    rows, width = LANES // 2, total.shape[1]
    arrays, layout = gathered(sources)

    def kernel(total_ref, *refs):
        send_ref, keep_ref, sum_ref = refs[-3:]
        sum_ref[...] = total_ref[...]
        add_chunks(sum_ref, chunks_of(refs[:-3], layout), False)
        mine = lax.axis_index("tile_0")
        send_ref[...] = sum_ref[pl.ds(pl.multiple_of((1 - mine) * rows, rows), rows), :]
        keep_ref[...] = sum_ref[pl.ds(pl.multiple_of(mine * rows, rows), rows), :]

    half = jax.ShapeDtypeStruct((rows, width), jnp.float32)
    return pl.pallas_call(
        kernel,
        out_shape=(half, half),
        in_specs=[VMEM] * (1 + len(arrays)),
        out_specs=(VMEM, VMEM),
        scratch_shapes=[pltpu.VMEM((LANES, width), jnp.float32)],
        compiler_params=PARAMS,
        name="last_chunks",
    )(total, *arrays)


def finish(result, stiff, product, chain):
    rows, width = product.shape
    given = [] if result is None else [result]

    def kernel(*refs):
        stiff_ref, product_ref, out_hbm, buf, sem = refs[len(given) :]
        slot = slot_of(chain)
        buf[...] = stiff_ref[slot] - product_ref[...]
        copy = pltpu.make_async_copy(buf, out_hbm.at[slot], sem)
        copy.start()
        copy.wait()

    return pl.pallas_call(
        kernel,
        out_shape=jax.ShapeDtypeStruct((OWN, rows, width), jnp.float32),
        in_specs=[HBM] * len(given) + [VMEM, VMEM],
        out_specs=HBM,
        scratch_shapes=[pltpu.VMEM((rows, width), jnp.float32), pltpu.SemaphoreType.DMA],
        input_output_aliases={0: 0} if given else {},
        compiler_params=PARAMS,
        name=f"finish_{chain}",
    )(*given, stiff, product)


def shifted(array, axis, distance):
    size = lax.axis_size(axis)
    return lax.ppermute(array, axis, [(i, (i + distance) % size) for i in range(size)])


def swapped(array, axis):
    return lax.ppermute(array, axis, [(i, i ^ 1) for i in range(lax.axis_size(axis))])


def after(array, *earlier):
    return lax.optimization_barrier((array, *earlier))[0]


def up(array):
    return shifted(array, "tile_1", 1)


def down(array):
    return shifted(array, "tile_1", -1)


def body(coupling, interior_solve, boundary_stiffness, migration):
    home, depth, width = interior_solve.shape
    blocks = width // LANES
    half = blocks // 2
    last = 2 * blocks - 1
    pieces = jnp.swapaxes(coupling, 1, 2)
    in_hbm = [pltpu.with_memory_space_constraint(a, pltpu.HBM) for a in (migration, pieces, interior_solve)]
    outgoing = pack(*in_hbm, True)
    arrived = [swapped(outgoing[0], "group"), swapped(outgoing[1], "group")]
    local = pack(migration, *in_hbm[1:], False)
    packet1 = swapped(merge(migration, arrived[1], local[1], 1, home), "tile_0")
    packet0 = merge(migration, arrived[0], local[0], 0, home)

    def run(first):
        return list(range(first, first + blocks))

    left = list(range(half))
    u0, d0 = up(packet0[0 : 4 + blocks]), down(packet0[4:last])
    stiff_arrived = swapped(stiff_out(after(migration, packet0), boundary_stiffness), "group")
    stiff = stiff_merge(migration, boundary_stiffness, stiff_arrived)
    u1, d1 = up(after(packet1[0 : 3 + blocks], u0, d0)), down(after(packet1[3:last], u0, d0))
    uu0, dd0 = up(after(u0[1:], stiff_arrived)), down(d0[:-1])
    total = accumulate(
        None, [(packet0, run(4), packet0, last), (u0, run(4), u0, 0), (d0, run(0), d0, blocks + 2)], width, "chunks_1"
    )
    uu1, dd1 = up(u1[1:]), down(d1[:-1])
    uuu0, ddd0 = up(after(uu0[1:], total)), down(dd0[:-1])
    total = accumulate(
        total,
        [(packet1, run(3), packet1, last), (u1, run(3), u1, 0), (d1, run(0), d1, blocks + 3)], width, "chunks_2",
    )
    uuu1, ddd1 = up(uu1[1:]), down(after(dd1[:-1], total))
    total = accumulate(
        total,
        [
            (uu0, run(3), uu0, 0), (dd0, run(0), dd0, blocks + 1),
            (uu1, run(2), uu1, 0), (dd1, run(0), dd1, blocks + 2),
        ],
        width, "chunks_3",
    )
    far0a, far0b = up(uuu0[1 : half + 2]), down(ddd0[half:blocks])
    far1a, far1b = up(uuu1[1 : half + 1]), down(after(ddd1[half : blocks + 1], total))
    total = accumulate(
        total,
        [
            (uuu0, run(2), uuu0, 0), (ddd0, run(0), ddd0, blocks),
            (uuu1, run(1), uuu1, 0), (ddd1, run(0), ddd1, blocks + 1),
        ],
        width, "chunks_4",
    )
    send, keep = last_chunks(
        total,
        [
            ((far0a, far0b), [1, 2, 3, 4, 0, 1, 2, 3], far0a, 0),
            ((far1a, far1b), left + left, far1b, half),
        ],
    )
    other = swapped(send, "tile_0")
    return finish(finish(None, stiff, keep, 0), stiff, other, 1)


def solution(mesh):
    finer = Mesh(mesh.devices.reshape(mesh.shape["group"], 2, 8), ("group", "tile_0", "tile_1"))
    in_specs = (P("group", None, TILE), P("group", TILE, None), P("group", TILE, None), P())
    out_specs = P("group", TILE, None)
    return jax.shard_map(body, mesh=finer, in_specs=in_specs, out_specs=out_specs, check_vma=False)
```

```python
import jax
import jax.numpy as jnp
from jax import lax
from jax.experimental import pallas as pl
from jax.experimental.pallas import tpu as pltpu
from jax.sharding import Mesh
from jax.sharding import PartitionSpec as P

OWN = 2
TILE = ("tile_0", "tile_1")
LANES = 128
PARAMS = pltpu.CompilerParams(vmem_limit_bytes=32 * 1024 * 1024)
SMEM = pl.BlockSpec(memory_space=pltpu.SMEM)
VMEM = pl.BlockSpec(memory_space=pltpu.VMEM)
HBM = pl.BlockSpec(memory_space=pltpu.HBM)


def hops(chain):
    return (4, 3) if chain == 0 else (3, 4)


def slot_of(chain):
    column = lax.axis_index("tile_0")
    return column if chain == 0 else 1 - column


def locate(plan, group, wanted, home):
    position, here = jnp.int32(0), jnp.bool_(False)
    for k in range(home):
        match = plan[group * home + k] == wanted
        position = jnp.where(match, jnp.int32(k), position)
        here = jnp.logical_or(here, match)
    return position, here


def pack(plan, coupling, solve, stiff=None):
    home, depth, width = solve.shape
    blocks = width // LANES
    for_partner = stiff is not None

    def kernel(plan_given, c_hbm, x_hbm, *refs):
        if for_partner:
            b_hbm, out0, out1, out_b, plan_buf, c_buf, x_buf, plan_sem, c_sem, x_sem, b_sem = refs
        else:
            out0, out1, c_buf, x_buf, c_sem, x_sem = refs
        group = lax.axis_index("group")
        place = lax.axis_index("tile_1")
        owner = jnp.bitwise_xor(group, 1) if for_partner else group
        outs = (out0, out1)
        copies = [
            pltpu.make_async_copy(c_hbm, c_buf, c_sem),
            pltpu.make_async_copy(x_hbm, x_buf, x_sem),
        ]
        for copy in copies:
            copy.start()
        plan_ref = plan_given
        if for_partner:
            plan_copy = pltpu.make_async_copy(plan_given, plan_buf, plan_sem)
            plan_copy.start()
            plan_ref = plan_buf
        low = lax.broadcasted_iota(jnp.int32, (depth, LANES), 1) < LANES // 2
        if for_partner:
            plan_copy.wait()
        positions = [locate(plan_ref, group, owner * OWN + slot_of(slot), home)[0] for slot in range(OWN)]
        b_copies = []
        if for_partner:
            for slot in range(OWN):
                place_b, _ = locate(plan_ref, group, owner * OWN + slot, home)
                b_copies.append(pltpu.make_async_copy(b_hbm.at[place_b], out_b.at[slot], b_sem.at[slot]))
                b_copies[slot].start()
        copies[0].wait()
        for slot in range(OWN):
            up = hops(slot)[0]
            for m in range(blocks // 2):
                first = c_buf[positions[slot], :, pl.ds(m * LANES, LANES)]
                second = c_buf[positions[slot], :, pl.ds((m + blocks // 2) * LANES, LANES)]
                even = jnp.where(low, first, pltpu.roll(second, LANES // 2, 1))
                odd = jnp.where(low, pltpu.roll(first, LANES // 2, 1), second)
                for to, piece in ((2 * m, even), (2 * m + 1, odd)):
                    ahead = jnp.bitwise_and(to - place, blocks - 1)
                    spot = jnp.where(ahead == 0, 15, jnp.where(ahead <= up, ahead - 1, ahead + 7))
                    outs[slot][spot] = piece
        copies[1].wait()
        for slot in range(OWN):
            up = hops(slot)[0]
            for n in range(blocks):
                outs[slot][up + n] = x_buf[positions[slot], :, pl.ds(n * LANES, LANES)]
        for copy in b_copies:
            copy.wait()

    packet = jax.ShapeDtypeStruct((2 * blocks, depth, LANES), jnp.float32)
    staging = [pltpu.VMEM((home, depth, width), jnp.float32)] * 2
    semaphores = [pltpu.SemaphoreType.DMA] * 2
    if not for_partner:
        return pl.pallas_call(
            kernel,
            out_shape=(packet, packet),
            in_specs=[SMEM, HBM, HBM],
            out_specs=(VMEM, VMEM),
            scratch_shapes=[*staging, *semaphores],
            compiler_params=PARAMS,
            name="pack_own",
        )(plan, coupling, solve)
    return pl.pallas_call(
        kernel,
        out_shape=(packet, packet, jax.ShapeDtypeStruct((OWN, *stiff.shape[1:]), jnp.float32)),
        in_specs=[HBM] * 4,
        out_specs=(VMEM, VMEM, VMEM),
        scratch_shapes=[
            pltpu.SMEM(plan.shape, jnp.int32),
            *staging,
            pltpu.SemaphoreType.DMA,
            *semaphores,
            pltpu.SemaphoreType.DMA((OWN,)),
        ],
        compiler_params=PARAMS,
        name="pack_partner",
    )(plan, coupling, solve, stiff)


def merge(plan, arrived, local, chain, home):
    total, depth, _ = arrived.shape
    up, down = hops(chain)
    blocks = total // 2

    def kernel(plan_ref, arrived_ref, local_ref, up_ref, down_ref, own_ref):
        group = lax.axis_index("group")
        _, here = locate(plan_ref, group, group * OWN + slot_of(chain), home)

        def put(source):
            up_ref[...] = source[0 : up + blocks]
            down_ref[...] = source[up : total - 1]
            if chain == 0:
                own_ref[0] = source[total - 1]
            else:
                own_ref[0:blocks] = source[up : up + blocks]
                own_ref[blocks] = source[total - 1]

        @pl.when(here)
        def _():
            put(local_ref)

        @pl.when(jnp.logical_not(here))
        def _():
            put(arrived_ref)

    return pl.pallas_call(
        kernel,
        out_shape=(
            jax.ShapeDtypeStruct((up + blocks, depth, LANES), jnp.float32),
            jax.ShapeDtypeStruct((down + blocks, depth, LANES), jnp.float32),
            jax.ShapeDtypeStruct((1 if chain == 0 else 1 + blocks, depth, LANES), jnp.float32),
        ),
        in_specs=[SMEM, VMEM, VMEM],
        out_specs=(VMEM, VMEM, VMEM),
        compiler_params=PARAMS,
        name=f"merge_{chain}",
    )(plan, arrived, local)


def stiff_merge(plan, stiff, arrived):
    home, rows, width = stiff.shape

    def kernel(plan_ref, b_hbm, arrived_ref, out_ref, sem):
        group = lax.axis_index("group")
        for slot in range(OWN):
            position, here = locate(plan_ref, group, group * OWN + slot, home)

            @pl.when(here)
            def _():
                copy = pltpu.make_async_copy(b_hbm.at[position], out_ref.at[slot], sem.at[slot])
                copy.start()
                copy.wait()

            @pl.when(jnp.logical_not(here))
            def _():
                out_ref[slot] = arrived_ref[slot]

    return pl.pallas_call(
        kernel,
        out_shape=jax.ShapeDtypeStruct((OWN, rows, width), jnp.float32),
        in_specs=[SMEM, HBM, VMEM],
        out_specs=VMEM,
        scratch_shapes=[pltpu.SemaphoreType.DMA((OWN,))],
        compiler_params=PARAMS,
        name="stiff_merge",
    )(plan, stiff, arrived)


def split(value):
    high = value.astype(jnp.bfloat16)
    return high, (value - high.astype(jnp.float32)).astype(jnp.bfloat16)


def add_chunks(total_ref, chunks, start):
    for packet, places, piece in chunks:
        c_high, c_low = split(piece)
        left = jnp.concatenate([c_high, c_high, c_low], axis=0)
        for n in range(0, len(places), 2):
            x = jnp.concatenate([packet[places[n]], packet[places[n + 1]]], axis=1)
            x_high, x_low = split(x)
            right = jnp.concatenate([x_high, x_low, x_high], axis=0)
            product = lax.dot_general(left, right, (((0,), (0,)), ((), ())), preferred_element_type=jnp.float32)
            where = (slice(None), pl.ds(n * LANES, 2 * LANES))
            total_ref[where] = product if start else total_ref[where] + product
        start = False


def gathered(sources):
    arrays, layout = [], []

    def place(array):
        for k, known in enumerate(arrays):
            if known is array:
                return k
        arrays.append(array)
        return len(arrays) - 1

    for packet, places, holder, index in sources:
        layout.append((place(packet), places, place(holder), index))
    return arrays, layout


def chunks_of(refs, layout):
    return [
        (refs[k], places, refs[holder][...] if index is None else refs[holder][index])
        for k, places, holder, index in layout
    ]


def accumulate(total, sources, width, name):
    arrays, layout = gathered(sources)
    given = [] if total is None else [total]
    n_given = len(given)

    def kernel(*refs):
        total_ref = refs[-1]
        if n_given:
            total_ref[...] = refs[0][...]
        add_chunks(total_ref, chunks_of(refs[n_given:-1], layout), not n_given)

    return pl.pallas_call(
        kernel,
        out_shape=jax.ShapeDtypeStruct((LANES, width), jnp.float32),
        in_specs=[VMEM] * (n_given + len(arrays)),
        out_specs=VMEM,
        input_output_aliases={0: 0} if n_given else {},
        compiler_params=PARAMS,
        cost_estimate=pl.CostEstimate(flops=2 * 144 * 128 * 1024, bytes_accessed=1 << 20, transcendentals=0),
        name=name,
    )(*given, *arrays)


def last_chunks(total, sources):
    rows, width = LANES // 2, total.shape[1]
    arrays, layout = gathered(sources)

    def kernel(total_ref, *refs):
        send_ref, keep_ref, sum_ref = refs[-3:]
        sum_ref[...] = total_ref[...]
        add_chunks(sum_ref, chunks_of(refs[:-3], layout), False)
        mine = lax.axis_index("tile_0")
        send_ref[...] = sum_ref[pl.ds(pl.multiple_of((1 - mine) * rows, rows), rows), :]
        keep_ref[...] = sum_ref[pl.ds(pl.multiple_of(mine * rows, rows), rows), :]

    half = jax.ShapeDtypeStruct((rows, width), jnp.float32)
    return pl.pallas_call(
        kernel,
        out_shape=(half, half),
        in_specs=[VMEM] * (1 + len(arrays)),
        out_specs=(VMEM, VMEM),
        scratch_shapes=[pltpu.VMEM((LANES, width), jnp.float32)],
        compiler_params=PARAMS,
        name="last_chunks",
    )(total, *arrays)


def finish(result, stiff, product, chain):
    rows, width = product.shape
    given = [] if result is None else [result]

    def kernel(*refs):
        stiff_ref, product_ref, out_hbm, buf, sem = refs[len(given) :]
        slot = slot_of(chain)
        buf[...] = stiff_ref[slot] - product_ref[...]
        copy = pltpu.make_async_copy(buf, out_hbm.at[slot], sem)
        copy.start()
        copy.wait()

    return pl.pallas_call(
        kernel,
        out_shape=jax.ShapeDtypeStruct((OWN, rows, width), jnp.float32),
        in_specs=[HBM] * len(given) + [VMEM, VMEM],
        out_specs=HBM,
        scratch_shapes=[pltpu.VMEM((rows, width), jnp.float32), pltpu.SemaphoreType.DMA],
        input_output_aliases={0: 0} if given else {},
        compiler_params=PARAMS,
        name=f"finish_{chain}",
    )(*given, stiff, product)


def shifted(array, axis, distance):
    size = lax.axis_size(axis)
    return lax.ppermute(array, axis, [(i, (i + distance) % size) for i in range(size)])


def swapped(array, axis):
    return lax.ppermute(array, axis, [(i, i ^ 1) for i in range(lax.axis_size(axis))])


def after(array, *earlier):
    return lax.optimization_barrier((array, *earlier))[0]


def crossed(array, distance):
    size = lax.axis_size("tile_1")
    pairs = [(x * size + z, (1 - x) * size + (z + distance) % size) for x in range(2) for z in range(size)]
    return lax.ppermute(array, TILE, pairs)


def body(coupling, interior_solve, boundary_stiffness, migration):
    home, depth, width = interior_solve.shape
    blocks = width // LANES
    pieces = jnp.swapaxes(coupling, 1, 2)
    in_hbm = [pltpu.with_memory_space_constraint(a, pltpu.HBM) for a in (migration, pieces, interior_solve, boundary_stiffness)]
    outgoing = pack(*in_hbm)
    arrived = [swapped(outgoing[0], "group"), swapped(outgoing[1], "group")]
    stiff_arrived = swapped(outgoing[2], "group")
    local = pack(migration, *in_hbm[1:3])
    ups, downs, owns = [None, None], [None, None], [None, None]
    for chain in range(2):
        ups[chain], downs[chain], owns[chain] = merge(migration, arrived[chain], local[chain], chain, home)
    stiff = stiff_merge(migration, boundary_stiffness, stiff_arrived)

    def run(first):
        return list(range(first, first + blocks))

    crossed_own = crossed(owns[1], 0)
    sources = [(ups[0], run(hops(0)[0]), owns[0], 0)]
    total = None
    for step in range(1, 4):
        for chain in range(2):
            if step == 1 and chain == 1:
                ups[chain] = crossed(after(ups[chain], stiff_arrived), 1)
                downs[chain] = crossed(downs[chain], -1)
            else:
                sent_up = ups[chain] if step == 1 else ups[chain][1:]
                sent_down = downs[chain] if step == 1 else downs[chain][:-1]
                ups[chain], downs[chain] = shifted(sent_up, "tile_1", 1), shifted(sent_down, "tile_1", -1)
        total = accumulate(total, sources, width, f"chunks_{step}")
        sources = [] if step > 1 else [(crossed_own, run(0), crossed_own, blocks)]
        for chain in range(2):
            left_up, left_down = hops(chain)[0] - step, hops(chain)[1] - step
            sources.append((ups[chain], run(left_up + 1), ups[chain], 0))
            sources.append((downs[chain], run(0), downs[chain], blocks + left_down))
    far0, far1 = shifted(ups[0][1:], "tile_1", 1), shifted(downs[1][:-1], "tile_1", -1)
    total = accumulate(total, sources, width, "chunks_4")
    send, keep = last_chunks(total, [(far0, run(1), far0, 0), (far1, run(0), far1, blocks)])
    other = swapped(send, "tile_0")
    return finish(finish(None, stiff, keep, 0), stiff, other, 1)


def solution(mesh):
    finer = Mesh(mesh.devices.reshape(mesh.shape["group"], 2, 8), ("group", "tile_0", "tile_1"))
    in_specs = (P("group", None, TILE), P("group", TILE, None), P("group", TILE, None), P())
    out_specs = P("group", TILE, None)
    return jax.shard_map(body, mesh=finer, in_specs=in_specs, out_specs=out_specs, check_vma=False)
```

```python
import jax
import jax.numpy as jnp
from jax import lax
from jax.experimental import pallas as pl
from jax.experimental.pallas import tpu as pltpu
from jax.sharding import Mesh
from jax.sharding import PartitionSpec as P

OWN = 2
TILE = ("tile_0", "tile_1")
LANES = 128
PARAMS = pltpu.CompilerParams(vmem_limit_bytes=32 * 1024 * 1024)
SMEM = pl.BlockSpec(memory_space=pltpu.SMEM)
VMEM = pl.BlockSpec(memory_space=pltpu.VMEM)
HBM = pl.BlockSpec(memory_space=pltpu.HBM)


def hops(chain):
    return (4, 3) if chain == 0 else (3, 4)


def slot_of(chain):
    column = lax.axis_index("tile_0")
    return column if chain == 0 else 1 - column


def locate(plan, group, wanted, home):
    position, here = jnp.int32(0), jnp.bool_(False)
    for k in range(home):
        match = plan[group * home + k] == wanted
        position = jnp.where(match, jnp.int32(k), position)
        here = jnp.logical_or(here, match)
    return position, here


def write_pieces(out, c_buf, position, chain, blocks):
    place = lax.axis_index("tile_1")
    low = lax.broadcasted_iota(jnp.int32, out.shape[1:], 1) < LANES // 2
    going_up = hops(chain)[0]
    for m in range(blocks // 2):
        first = c_buf[position, :, pl.ds(m * LANES, LANES)]
        second = c_buf[position, :, pl.ds((m + blocks // 2) * LANES, LANES)]
        even = jnp.where(low, first, pltpu.roll(second, LANES // 2, 1))
        odd = jnp.where(low, pltpu.roll(first, LANES // 2, 1), second)
        for to, piece in ((2 * m, even), (2 * m + 1, odd)):
            ahead = jnp.bitwise_and(to - place, blocks - 1)
            out[jnp.where(ahead == 0, 15, jnp.where(ahead <= going_up, ahead - 1, ahead + 7))] = piece


def write_panel(out, x_buf, position, chain, blocks):
    going_up = hops(chain)[0]
    for n in range(blocks):
        out[going_up + n] = x_buf[position, :, pl.ds(n * LANES, LANES)]


def find(plan, wanted, home):
    position, here = jnp.int32(0), jnp.bool_(False)
    for k in range(home):
        match = plan[k] == wanted
        position = jnp.where(match, jnp.int32(k), position)
        here = jnp.logical_or(here, match)
    return position, here


def pack_partner(plan, coupling, solve):
    home, depth, width = solve.shape
    blocks = width // LANES

    def kernel(plan_hbm, c_hbm, x_hbm, out0, out1, c_buf, x_buf, plan_out, plan_ref, plan_sem, c_sem, x_sem):
        group = lax.axis_index("group")
        plan_copy = pltpu.make_async_copy(plan_hbm, plan_ref, plan_sem)
        c_copy = pltpu.make_async_copy(c_hbm, c_buf, c_sem)
        x_copy = pltpu.make_async_copy(x_hbm, x_buf, x_sem)
        plan_copy.start()
        c_copy.start()
        x_copy.start()
        plan_copy.wait()
        for k in range(home):
            plan_out[k] = plan_ref[group * home + k]
        partner = jnp.bitwise_xor(group, 1)
        positions = [locate(plan_ref, group, partner * OWN + slot_of(chain), home)[0] for chain in range(2)]
        c_copy.wait()
        for chain, out in enumerate((out0, out1)):
            write_pieces(out, c_buf, positions[chain], chain, blocks)
        x_copy.wait()
        for chain, out in enumerate((out0, out1)):
            write_panel(out, x_buf, positions[chain], chain, blocks)

    packet = jax.ShapeDtypeStruct((2 * blocks, depth, LANES), jnp.float32)
    staging = jax.ShapeDtypeStruct(solve.shape, jnp.float32)
    return pl.pallas_call(
        kernel,
        out_shape=(packet, packet, staging, staging, jax.ShapeDtypeStruct((home,), jnp.int32)),
        in_specs=[HBM] * 3,
        out_specs=(VMEM, VMEM, VMEM, VMEM, SMEM),
        scratch_shapes=[pltpu.SMEM(plan.shape, jnp.int32)] + [pltpu.SemaphoreType.DMA] * 3,
        compiler_params=PARAMS,
        name="pack_partner",
    )(plan, coupling, solve)


def merge(plan, arrived, coupling, solve, chain):
    total, depth, _ = arrived.shape
    up, down = hops(chain)
    blocks = total // 2
    home = solve.shape[0]

    def kernel(plan_ref, arrived_ref, c_ref, x_ref, up_ref, down_ref, own_ref, packed):
        group = lax.axis_index("group")
        position, here = find(plan_ref, group * OWN + slot_of(chain), home)

        def put(source):
            up_ref[...] = source[0 : up + blocks]
            down_ref[...] = source[up : total - 1]
            if chain == 0:
                own_ref[0] = source[total - 1]
            else:
                own_ref[0:blocks] = source[up : up + blocks]
                own_ref[blocks] = source[total - 1]

        @pl.when(here)
        def _():
            write_pieces(packed, c_ref, position, chain, blocks)
            write_panel(packed, x_ref, position, chain, blocks)
            put(packed)

        @pl.when(jnp.logical_not(here))
        def _():
            put(arrived_ref)

    return pl.pallas_call(
        kernel,
        out_shape=(
            jax.ShapeDtypeStruct((up + blocks, depth, LANES), jnp.float32),
            jax.ShapeDtypeStruct((down + blocks, depth, LANES), jnp.float32),
            jax.ShapeDtypeStruct((1 if chain == 0 else 1 + blocks, depth, LANES), jnp.float32),
        ),
        in_specs=[SMEM, VMEM, VMEM, VMEM],
        out_specs=(VMEM, VMEM, VMEM),
        scratch_shapes=[pltpu.VMEM(arrived.shape, jnp.float32)],
        compiler_params=PARAMS,
        name=f"merge_{chain}",
    )(plan, arrived, coupling, solve)


def stiff_out(plan, stiff):
    home, rows, width = stiff.shape

    def kernel(plan_ref, b_hbm, out_ref, sem):
        group = lax.axis_index("group")
        copies = []
        for slot in range(OWN):
            position, _ = locate(plan_ref, group, jnp.bitwise_xor(group, 1) * OWN + slot, home)
            copy = pltpu.make_async_copy(b_hbm.at[position], out_ref.at[slot], sem.at[slot])
            copy.start()
            copies.append(copy)
        for copy in copies:
            copy.wait()

    return pl.pallas_call(
        kernel,
        out_shape=jax.ShapeDtypeStruct((OWN, rows, width), jnp.float32),
        in_specs=[SMEM, HBM],
        out_specs=VMEM,
        scratch_shapes=[pltpu.SemaphoreType.DMA((OWN,))],
        compiler_params=PARAMS,
        name="stiff_out",
    )(plan, stiff)


def stiff_merge(plan, stiff, arrived):
    home, rows, width = stiff.shape

    def kernel(plan_ref, b_hbm, arrived_ref, out_ref, sem):
        group = lax.axis_index("group")
        for slot in range(OWN):
            position, here = locate(plan_ref, group, group * OWN + slot, home)

            @pl.when(here)
            def _():
                copy = pltpu.make_async_copy(b_hbm.at[position], out_ref.at[slot], sem.at[slot])
                copy.start()
                copy.wait()

            @pl.when(jnp.logical_not(here))
            def _():
                out_ref[slot] = arrived_ref[slot]

    return pl.pallas_call(
        kernel,
        out_shape=jax.ShapeDtypeStruct((OWN, rows, width), jnp.float32),
        in_specs=[SMEM, HBM, VMEM],
        out_specs=VMEM,
        scratch_shapes=[pltpu.SemaphoreType.DMA((OWN,))],
        compiler_params=PARAMS,
        name="stiff_merge",
    )(plan, stiff, arrived)


def split(value):
    high = value.astype(jnp.bfloat16)
    return high, (value - high.astype(jnp.float32)).astype(jnp.bfloat16)


def add_chunks(total_ref, chunks, start):
    for packet, places, piece in chunks:
        c_high, c_low = split(piece)
        left = jnp.concatenate([c_high, c_high, c_low], axis=0)
        for n in range(0, len(places), 2):
            x = jnp.concatenate([packet[places[n]], packet[places[n + 1]]], axis=1)
            x_high, x_low = split(x)
            right = jnp.concatenate([x_high, x_low, x_high], axis=0)
            product = lax.dot_general(left, right, (((0,), (0,)), ((), ())), preferred_element_type=jnp.float32)
            where = (slice(None), pl.ds(n * LANES, 2 * LANES))
            total_ref[where] = product if start else total_ref[where] + product
        start = False


def gathered(sources):
    arrays, layout = [], []

    def place(array):
        for k, known in enumerate(arrays):
            if known is array:
                return k
        arrays.append(array)
        return len(arrays) - 1

    for packet, places, holder, index in sources:
        layout.append((place(packet), places, place(holder), index))
    return arrays, layout


def chunks_of(refs, layout):
    return [
        (refs[k], places, refs[holder][...] if index is None else refs[holder][index])
        for k, places, holder, index in layout
    ]


def accumulate(total, sources, width, name):
    arrays, layout = gathered(sources)
    given = [] if total is None else [total]
    n_given = len(given)

    def kernel(*refs):
        total_ref = refs[-1]
        if n_given:
            total_ref[...] = refs[0][...]
        add_chunks(total_ref, chunks_of(refs[n_given:-1], layout), not n_given)

    return pl.pallas_call(
        kernel,
        out_shape=jax.ShapeDtypeStruct((LANES, width), jnp.float32),
        in_specs=[VMEM] * (n_given + len(arrays)),
        out_specs=VMEM,
        input_output_aliases={0: 0} if n_given else {},
        compiler_params=PARAMS,
        cost_estimate=pl.CostEstimate(flops=2 * 144 * 128 * 1024, bytes_accessed=1 << 20, transcendentals=0),
        name=name,
    )(*given, *arrays)


def last_chunks(total, sources):
    rows, width = LANES // 2, total.shape[1]
    arrays, layout = gathered(sources)

    def kernel(total_ref, *refs):
        send_ref, keep_ref, sum_ref = refs[-3:]
        sum_ref[...] = total_ref[...]
        add_chunks(sum_ref, chunks_of(refs[:-3], layout), False)
        mine = lax.axis_index("tile_0")
        send_ref[...] = sum_ref[pl.ds(pl.multiple_of((1 - mine) * rows, rows), rows), :]
        keep_ref[...] = sum_ref[pl.ds(pl.multiple_of(mine * rows, rows), rows), :]

    half = jax.ShapeDtypeStruct((rows, width), jnp.float32)
    return pl.pallas_call(
        kernel,
        out_shape=(half, half),
        in_specs=[VMEM] * (1 + len(arrays)),
        out_specs=(VMEM, VMEM),
        scratch_shapes=[pltpu.VMEM((LANES, width), jnp.float32)],
        compiler_params=PARAMS,
        name="last_chunks",
    )(total, *arrays)


def finish(result, stiff, product, chain):
    rows, width = product.shape
    given = [] if result is None else [result]

    def kernel(*refs):
        stiff_ref, product_ref, out_hbm, buf, sem = refs[len(given) :]
        slot = slot_of(chain)
        buf[...] = stiff_ref[slot] - product_ref[...]
        copy = pltpu.make_async_copy(buf, out_hbm.at[slot], sem)
        copy.start()
        copy.wait()

    return pl.pallas_call(
        kernel,
        out_shape=jax.ShapeDtypeStruct((OWN, rows, width), jnp.float32),
        in_specs=[HBM] * len(given) + [VMEM, VMEM],
        out_specs=HBM,
        scratch_shapes=[pltpu.VMEM((rows, width), jnp.float32), pltpu.SemaphoreType.DMA],
        input_output_aliases={0: 0} if given else {},
        compiler_params=PARAMS,
        name=f"finish_{chain}",
    )(*given, stiff, product)


def shifted(array, axis, distance):
    size = lax.axis_size(axis)
    return lax.ppermute(array, axis, [(i, (i + distance) % size) for i in range(size)])


def swapped(array, axis):
    return lax.ppermute(array, axis, [(i, i ^ 1) for i in range(lax.axis_size(axis))])


def after(array, *earlier):
    return lax.optimization_barrier((array, *earlier))[0]


def crossed(array, distance):
    size = lax.axis_size("tile_1")
    pairs = [(x * size + z, (1 - x) * size + (z + distance) % size) for x in range(2) for z in range(size)]
    return lax.ppermute(array, TILE, pairs)


def body(coupling, interior_solve, boundary_stiffness, migration):
    home, depth, width = interior_solve.shape
    blocks = width // LANES
    pieces = jnp.swapaxes(coupling, 1, 2)
    in_hbm = [pltpu.with_memory_space_constraint(a, pltpu.HBM) for a in (migration, pieces, interior_solve)]
    out0, out1, c_home, x_home, home_plan = pack_partner(*in_hbm)
    arrived = [swapped(out0, "group"), swapped(out1, "group")]
    ups, downs, owns = [None, None], [None, None], [None, None]
    for chain in range(2):
        ups[chain], downs[chain], owns[chain] = merge(home_plan, arrived[chain], c_home, x_home, chain)
    stiff_arrived = swapped(stiff_out(migration, boundary_stiffness), "group")
    stiff = stiff_merge(migration, boundary_stiffness, stiff_arrived)

    def run(first):
        return list(range(first, first + blocks))

    crossed_own = crossed(owns[1], 0)
    sources = [(ups[0], run(hops(0)[0]), owns[0], 0)]
    total = None
    for step in range(1, 4):
        for chain in range(2):
            if step == 1 and chain == 1:
                ups[chain], downs[chain] = crossed(ups[chain], 1), crossed(downs[chain], -1)
            else:
                sent_up = ups[chain] if step == 1 else ups[chain][1:]
                sent_down = downs[chain] if step == 1 else downs[chain][:-1]
                ups[chain], downs[chain] = shifted(sent_up, "tile_1", 1), shifted(sent_down, "tile_1", -1)
        total = accumulate(total, sources, width, f"chunks_{step}")
        sources = [] if step > 1 else [(crossed_own, run(0), crossed_own, blocks)]
        for chain in range(2):
            left_up, left_down = hops(chain)[0] - step, hops(chain)[1] - step
            sources.append((ups[chain], run(left_up + 1), ups[chain], 0))
            sources.append((downs[chain], run(0), downs[chain], blocks + left_down))
    far0, far1 = shifted(ups[0][1:], "tile_1", 1), shifted(downs[1][:-1], "tile_1", -1)
    total = accumulate(total, sources, width, "chunks_4")
    send, keep = last_chunks(total, [(far0, run(1), far0, 0), (far1, run(0), far1, blocks)])
    other = swapped(send, "tile_0")
    return finish(finish(None, stiff, keep, 0), stiff, other, 1)


def solution(mesh):
    finer = Mesh(mesh.devices.reshape(mesh.shape["group"], 2, 8), ("group", "tile_0", "tile_1"))
    in_specs = (P("group", None, TILE), P("group", TILE, None), P("group", TILE, None), P())
    out_specs = P("group", TILE, None)
    return jax.shard_map(body, mesh=finer, in_specs=in_specs, out_specs=out_specs, check_vma=False)
```

```python
import jax
import jax.numpy as jnp
from jax import lax
from jax.experimental import pallas as pl
from jax.experimental.pallas import tpu as pltpu
from jax.sharding import Mesh
from jax.sharding import PartitionSpec as P

OWN = 2
TILE = ("tile_0", "tile_1")
LANES = 128
PARAMS = pltpu.CompilerParams(vmem_limit_bytes=32 * 1024 * 1024)
SMEM = pl.BlockSpec(memory_space=pltpu.SMEM)
VMEM = pl.BlockSpec(memory_space=pltpu.VMEM)
HBM = pl.BlockSpec(memory_space=pltpu.HBM)


def hops(chain):
    return (4, 3) if chain == 0 else (3, 4)


def slot_of(chain):
    column = lax.axis_index("tile_0")
    return column if chain == 0 else 1 - column


def locate(plan, group, wanted, home):
    position, here = jnp.int32(0), jnp.bool_(False)
    for k in range(home):
        match = plan[group * home + k] == wanted
        position = jnp.where(match, jnp.int32(k), position)
        here = jnp.logical_or(here, match)
    return position, here


def pack(plan, coupling, solve, for_partner):
    home, depth, width = solve.shape
    blocks = width // LANES

    def kernel(plan_hbm, c_hbm, x_hbm, out0, out1, *refs):
        plan_ref, c_buf, x_buf, plan_sem, c_sem, x_sem = refs[-6:]
        group = lax.axis_index("group")
        place = lax.axis_index("tile_1")
        owner = jnp.bitwise_xor(group, 1) if for_partner else group
        outs = (out0, out1)
        copies = [
            pltpu.make_async_copy(plan_hbm, plan_ref, plan_sem),
            pltpu.make_async_copy(c_hbm, c_buf, c_sem),
            pltpu.make_async_copy(x_hbm, x_buf, x_sem),
        ]
        for copy in copies:
            copy.start()
        low = lax.broadcasted_iota(jnp.int32, (depth, LANES), 1) < LANES // 2
        copies[0].wait()
        positions = [locate(plan_ref, group, owner * OWN + slot_of(slot), home)[0] for slot in range(OWN)]
        if for_partner:
            for chain in range(2):
                _, here = locate(plan_ref, group, group * OWN + slot_of(chain), home)
                refs[0][chain] = jnp.broadcast_to(here.astype(jnp.int32), refs[0].shape[1:])
        copies[1].wait()
        for slot in range(OWN):
            up = hops(slot)[0]
            for m in range(blocks // 2):
                first = c_buf[positions[slot], :, pl.ds(m * LANES, LANES)]
                second = c_buf[positions[slot], :, pl.ds((m + blocks // 2) * LANES, LANES)]
                even = jnp.where(low, first, pltpu.roll(second, LANES // 2, 1))
                odd = jnp.where(low, pltpu.roll(first, LANES // 2, 1), second)
                for to, piece in ((2 * m, even), (2 * m + 1, odd)):
                    ahead = jnp.bitwise_and(to - place, blocks - 1)
                    spot = jnp.where(ahead == 0, 15, jnp.where(ahead <= up, ahead - 1, ahead + 7))
                    outs[slot][spot] = piece
        copies[2].wait()
        for slot in range(OWN):
            up = hops(slot)[0]
            for n in range(blocks):
                outs[slot][up + n] = x_buf[positions[slot], :, pl.ds(n * LANES, LANES)]

    packet = jax.ShapeDtypeStruct((2 * blocks, depth, LANES), jnp.float32)
    return pl.pallas_call(
        kernel,
        out_shape=(packet, packet) + ((jax.ShapeDtypeStruct((2, 8, LANES), jnp.int32),) if for_partner else ()),
        in_specs=[HBM] * 3,
        out_specs=(VMEM, VMEM) + ((VMEM,) if for_partner else ()),
        scratch_shapes=[
            pltpu.SMEM(plan.shape, jnp.int32),
            pltpu.VMEM((home, depth, width), jnp.float32),
            pltpu.VMEM((home, depth, width), jnp.float32),
            pltpu.SemaphoreType.DMA,
            pltpu.SemaphoreType.DMA,
            pltpu.SemaphoreType.DMA,
        ],
        compiler_params=PARAMS,
        name="pack_partner" if for_partner else "pack_own",
    )(plan, coupling, solve)


def merge(at_home, arrived, local, chain):
    total, depth, _ = arrived.shape
    up, down = hops(chain)
    blocks = total // 2

    def kernel(home_ref, arrived_ref, local_ref, up_ref, down_ref, own_ref):
        here = jnp.broadcast_to(home_ref[chain, 0:1, :], (depth, LANES)) != 0
        for k in range(total):
            block = jnp.where(here, local_ref[k], arrived_ref[k])
            if k < up + blocks:
                up_ref[k] = block
            if up <= k < total - 1:
                down_ref[k - up] = block
            if chain == 1 and up <= k < up + blocks:
                own_ref[k - up] = block
            if k == total - 1:
                own_ref[blocks if chain else 0] = block

    return pl.pallas_call(
        kernel,
        out_shape=(
            jax.ShapeDtypeStruct((up + blocks, depth, LANES), jnp.float32),
            jax.ShapeDtypeStruct((down + blocks, depth, LANES), jnp.float32),
            jax.ShapeDtypeStruct((1 if chain == 0 else 1 + blocks, depth, LANES), jnp.float32),
        ),
        in_specs=[VMEM, VMEM, VMEM],
        out_specs=(VMEM, VMEM, VMEM),
        compiler_params=PARAMS,
        name=f"merge_{chain}",
    )(at_home, arrived, local)


def stiff_out(plan, stiff):
    home, rows, width = stiff.shape

    def kernel(plan_ref, b_hbm, out_ref, sem):
        group = lax.axis_index("group")
        copies = []
        for slot in range(OWN):
            position, _ = locate(plan_ref, group, jnp.bitwise_xor(group, 1) * OWN + slot, home)
            copy = pltpu.make_async_copy(b_hbm.at[position], out_ref.at[slot], sem.at[slot])
            copy.start()
            copies.append(copy)
        for copy in copies:
            copy.wait()

    return pl.pallas_call(
        kernel,
        out_shape=jax.ShapeDtypeStruct((OWN, rows, width), jnp.float32),
        in_specs=[SMEM, HBM],
        out_specs=VMEM,
        scratch_shapes=[pltpu.SemaphoreType.DMA((OWN,))],
        compiler_params=PARAMS,
        name="stiff_out",
    )(plan, stiff)


def stiff_merge(plan, stiff, arrived):
    home, rows, width = stiff.shape

    def kernel(plan_ref, b_hbm, arrived_ref, out_ref, sem):
        group = lax.axis_index("group")
        for slot in range(OWN):
            position, here = locate(plan_ref, group, group * OWN + slot, home)

            @pl.when(here)
            def _():
                copy = pltpu.make_async_copy(b_hbm.at[position], out_ref.at[slot], sem.at[slot])
                copy.start()
                copy.wait()

            @pl.when(jnp.logical_not(here))
            def _():
                out_ref[slot] = arrived_ref[slot]

    return pl.pallas_call(
        kernel,
        out_shape=jax.ShapeDtypeStruct((OWN, rows, width), jnp.float32),
        in_specs=[SMEM, HBM, VMEM],
        out_specs=VMEM,
        scratch_shapes=[pltpu.SemaphoreType.DMA((OWN,))],
        compiler_params=PARAMS,
        name="stiff_merge",
    )(plan, stiff, arrived)


def split(value):
    high = value.astype(jnp.bfloat16)
    return high, (value - high.astype(jnp.float32)).astype(jnp.bfloat16)


def add_chunks(total_ref, chunks, start):
    for packet, places, piece in chunks:
        c_high, c_low = split(piece)
        left = jnp.concatenate([c_high, c_high, c_low], axis=0)
        for n in range(0, len(places), 2):
            x = jnp.concatenate([packet[places[n]], packet[places[n + 1]]], axis=1)
            x_high, x_low = split(x)
            right = jnp.concatenate([x_high, x_low, x_high], axis=0)
            product = lax.dot_general(left, right, (((0,), (0,)), ((), ())), preferred_element_type=jnp.float32)
            where = (slice(None), pl.ds(n * LANES, 2 * LANES))
            total_ref[where] = product if start else total_ref[where] + product
        start = False


def gathered(sources):
    arrays, layout = [], []

    def place(array):
        for k, known in enumerate(arrays):
            if known is array:
                return k
        arrays.append(array)
        return len(arrays) - 1

    for packet, places, holder, index in sources:
        layout.append((place(packet), places, place(holder), index))
    return arrays, layout


def chunks_of(refs, layout):
    return [
        (refs[k], places, refs[holder][...] if index is None else refs[holder][index])
        for k, places, holder, index in layout
    ]


def accumulate(total, sources, width, name):
    arrays, layout = gathered(sources)
    given = [] if total is None else [total]
    n_given = len(given)

    def kernel(*refs):
        total_ref = refs[-1]
        if n_given:
            total_ref[...] = refs[0][...]
        add_chunks(total_ref, chunks_of(refs[n_given:-1], layout), not n_given)

    return pl.pallas_call(
        kernel,
        out_shape=jax.ShapeDtypeStruct((LANES, width), jnp.float32),
        in_specs=[VMEM] * (n_given + len(arrays)),
        out_specs=VMEM,
        input_output_aliases={0: 0} if n_given else {},
        compiler_params=PARAMS,
        cost_estimate=pl.CostEstimate(flops=2 * 144 * 128 * 1024, bytes_accessed=1 << 20, transcendentals=0),
        name=name,
    )(*given, *arrays)


def last_chunks(total, sources):
    rows, width = LANES // 2, total.shape[1]
    arrays, layout = gathered(sources)

    def kernel(total_ref, *refs):
        send_ref, keep_ref, sum_ref = refs[-3:]
        sum_ref[...] = total_ref[...]
        add_chunks(sum_ref, chunks_of(refs[:-3], layout), False)
        mine = lax.axis_index("tile_0")
        send_ref[...] = sum_ref[pl.ds(pl.multiple_of((1 - mine) * rows, rows), rows), :]
        keep_ref[...] = sum_ref[pl.ds(pl.multiple_of(mine * rows, rows), rows), :]

    half = jax.ShapeDtypeStruct((rows, width), jnp.float32)
    return pl.pallas_call(
        kernel,
        out_shape=(half, half),
        in_specs=[VMEM] * (1 + len(arrays)),
        out_specs=(VMEM, VMEM),
        scratch_shapes=[pltpu.VMEM((LANES, width), jnp.float32)],
        compiler_params=PARAMS,
        name="last_chunks",
    )(total, *arrays)


def finish(result, stiff, product, chain):
    rows, width = product.shape
    given = [] if result is None else [result]

    def kernel(*refs):
        stiff_ref, product_ref, out_hbm, buf, sem = refs[len(given) :]
        slot = slot_of(chain)
        buf[...] = stiff_ref[slot] - product_ref[...]
        copy = pltpu.make_async_copy(buf, out_hbm.at[slot], sem)
        copy.start()
        copy.wait()

    return pl.pallas_call(
        kernel,
        out_shape=jax.ShapeDtypeStruct((OWN, rows, width), jnp.float32),
        in_specs=[HBM] * len(given) + [VMEM, VMEM],
        out_specs=HBM,
        scratch_shapes=[pltpu.VMEM((rows, width), jnp.float32), pltpu.SemaphoreType.DMA],
        input_output_aliases={0: 0} if given else {},
        compiler_params=PARAMS,
        name=f"finish_{chain}",
    )(*given, stiff, product)


def shifted(array, axis, distance):
    size = lax.axis_size(axis)
    return lax.ppermute(array, axis, [(i, (i + distance) % size) for i in range(size)])


def swapped(array, axis):
    return lax.ppermute(array, axis, [(i, i ^ 1) for i in range(lax.axis_size(axis))])


def crossed(array, distance):
    size = lax.axis_size("tile_1")
    pairs = [(x * size + z, (1 - x) * size + (z + distance) % size) for x in range(2) for z in range(size)]
    return lax.ppermute(array, TILE, pairs)


def body(coupling, interior_solve, boundary_stiffness, migration):
    home, depth, width = interior_solve.shape
    blocks = width // LANES
    pieces = jnp.swapaxes(coupling, 1, 2)
    in_hbm = [pltpu.with_memory_space_constraint(a, pltpu.HBM) for a in (migration, pieces, interior_solve)]
    outgoing = pack(*in_hbm, True)
    arrived = [swapped(outgoing[0], "group"), swapped(outgoing[1], "group")]
    local = pack(*in_hbm, False)
    ups, downs, owns = [None, None], [None, None], [None, None]
    for chain in range(2):
        ups[chain], downs[chain], owns[chain] = merge(outgoing[2], arrived[chain], local[chain], chain)
    stiff_arrived = swapped(stiff_out(migration, boundary_stiffness), "group")
    stiff = stiff_merge(migration, boundary_stiffness, stiff_arrived)

    def run(first):
        return list(range(first, first + blocks))

    crossed_own = crossed(owns[1], 0)
    sources = [(ups[0], run(hops(0)[0]), owns[0], 0)]
    total = None
    for step in range(1, 4):
        for chain in range(2):
            if step == 1 and chain == 1:
                ups[chain], downs[chain] = crossed(ups[chain], 1), crossed(downs[chain], -1)
            else:
                sent_up = ups[chain] if step == 1 else ups[chain][1:]
                sent_down = downs[chain] if step == 1 else downs[chain][:-1]
                ups[chain], downs[chain] = shifted(sent_up, "tile_1", 1), shifted(sent_down, "tile_1", -1)
        total = accumulate(total, sources, width, f"chunks_{step}")
        sources = [] if step > 1 else [(crossed_own, run(0), crossed_own, blocks)]
        for chain in range(2):
            left_up, left_down = hops(chain)[0] - step, hops(chain)[1] - step
            sources.append((ups[chain], run(left_up + 1), ups[chain], 0))
            sources.append((downs[chain], run(0), downs[chain], blocks + left_down))
    far0, far1 = shifted(ups[0][1:], "tile_1", 1), shifted(downs[1][:-1], "tile_1", -1)
    total = accumulate(total, sources, width, "chunks_4")
    send, keep = last_chunks(total, [(far0, run(1), far0, 0), (far1, run(0), far1, blocks)])
    other = swapped(send, "tile_0")
    return finish(finish(None, stiff, keep, 0), stiff, other, 1)


def solution(mesh):
    finer = Mesh(mesh.devices.reshape(mesh.shape["group"], 2, 8), ("group", "tile_0", "tile_1"))
    in_specs = (P("group", None, TILE), P("group", TILE, None), P("group", TILE, None), P())
    out_specs = P("group", TILE, None)
    return jax.shard_map(body, mesh=finer, in_specs=in_specs, out_specs=out_specs, check_vma=False)
```

```python
import jax
import jax.numpy as jnp
from jax import lax
from jax.experimental import pallas as pl
from jax.experimental.pallas import tpu as pltpu
from jax.sharding import Mesh
from jax.sharding import PartitionSpec as P

OWN = 2
TILE = ("tile_0", "tile_1")
LANES = 128
PARAMS = pltpu.CompilerParams(vmem_limit_bytes=32 * 1024 * 1024)
SMEM = pl.BlockSpec(memory_space=pltpu.SMEM)
VMEM = pl.BlockSpec(memory_space=pltpu.VMEM)
HBM = pl.BlockSpec(memory_space=pltpu.HBM)


def hops(chain):
    return (3, 4) if chain == 0 else (4, 3)


def slot_of(chain):
    column = lax.axis_index("tile_0")
    return column if chain == 0 else 1 - column


def locate(plan, group, wanted, home):
    position, here = jnp.int32(0), jnp.bool_(False)
    for k in range(home):
        match = plan[group * home + k] == wanted
        position = jnp.where(match, jnp.int32(k), position)
        here = jnp.logical_or(here, match)
    return position, here


def pack(plan, coupling, solve, for_partner):
    home, depth, width = solve.shape
    blocks = width // LANES

    def kernel(plan_hbm, c_hbm, x_hbm, out0, out1, *refs):
        plan_ref, c_buf, x_buf, plan_sem, c_sem, x_sem = refs[-6:]
        group = lax.axis_index("group")
        place = lax.axis_index("tile_1")
        owner = jnp.bitwise_xor(group, 1) if for_partner else group
        outs = (out0, out1)
        copies = [
            pltpu.make_async_copy(plan_hbm, plan_ref, plan_sem),
            pltpu.make_async_copy(c_hbm, c_buf, c_sem),
            pltpu.make_async_copy(x_hbm, x_buf, x_sem),
        ]
        for copy in copies:
            copy.start()
        low = lax.broadcasted_iota(jnp.int32, (depth, LANES), 1) < LANES // 2
        copies[0].wait()
        positions = [locate(plan_ref, group, owner * OWN + slot_of(slot), home)[0] for slot in range(OWN)]
        if for_partner:
            for chain in range(2):
                _, here = locate(plan_ref, group, group * OWN + slot_of(chain), home)
                refs[0][chain] = jnp.broadcast_to(here.astype(jnp.int32), refs[0].shape[1:])
        copies[1].wait()
        for slot in range(OWN):
            up = hops(slot)[0]
            for m in range(blocks // 2):
                first = c_buf[positions[slot], :, pl.ds(m * LANES, LANES)]
                second = c_buf[positions[slot], :, pl.ds((m + blocks // 2) * LANES, LANES)]
                even = jnp.where(low, first, pltpu.roll(second, LANES // 2, 1))
                odd = jnp.where(low, pltpu.roll(first, LANES // 2, 1), second)
                for to, piece in ((2 * m, even), (2 * m + 1, odd)):
                    ahead = jnp.bitwise_and(to - place, blocks - 1)
                    spot = jnp.where(ahead == 0, 15, jnp.where(ahead <= up, ahead - 1, ahead + 7))
                    outs[slot][spot] = piece
        copies[2].wait()
        for slot in range(OWN):
            up = hops(slot)[0]
            for n in range(blocks):
                outs[slot][up + n] = x_buf[positions[slot], :, pl.ds(n * LANES, LANES)]

    packet = jax.ShapeDtypeStruct((2 * blocks, depth, LANES), jnp.float32)
    return pl.pallas_call(
        kernel,
        out_shape=(packet, packet) + ((jax.ShapeDtypeStruct((2, 8, LANES), jnp.int32),) if for_partner else ()),
        in_specs=[HBM] * 3,
        out_specs=(VMEM, VMEM) + ((VMEM,) if for_partner else ()),
        scratch_shapes=[
            pltpu.SMEM(plan.shape, jnp.int32),
            pltpu.VMEM((home, depth, width), jnp.float32),
            pltpu.VMEM((home, depth, width), jnp.float32),
            pltpu.SemaphoreType.DMA,
            pltpu.SemaphoreType.DMA,
            pltpu.SemaphoreType.DMA,
        ],
        compiler_params=PARAMS,
        name="pack_partner" if for_partner else "pack_own",
    )(plan, coupling, solve)


def merge(at_home, arrived, local, chain):
    total, depth, _ = arrived.shape
    up, down = hops(chain)
    blocks = total // 2

    def kernel(home_ref, arrived_ref, local_ref, up_ref, down_ref, own_ref):
        here = jnp.broadcast_to(home_ref[chain, 0:1, :], (depth, LANES)) != 0
        for k in range(total):
            block = jnp.where(here, local_ref[k], arrived_ref[k])
            if k < up + blocks:
                up_ref[k] = block
            if up <= k < total - 1:
                down_ref[k - up] = block
            if chain == 1 and up <= k < up + blocks:
                own_ref[k - up] = block
            if k == total - 1:
                own_ref[blocks if chain else 0] = block

    return pl.pallas_call(
        kernel,
        out_shape=(
            jax.ShapeDtypeStruct((up + blocks, depth, LANES), jnp.float32),
            jax.ShapeDtypeStruct((down + blocks, depth, LANES), jnp.float32),
            jax.ShapeDtypeStruct((1 if chain == 0 else 1 + blocks, depth, LANES), jnp.float32),
        ),
        in_specs=[VMEM, VMEM, VMEM],
        out_specs=(VMEM, VMEM, VMEM),
        compiler_params=PARAMS,
        name=f"merge_{chain}",
    )(at_home, arrived, local)


def stiff_out(plan, stiff):
    home, rows, width = stiff.shape

    def kernel(plan_ref, b_hbm, out_ref, sem):
        group = lax.axis_index("group")
        copies = []
        for slot in range(OWN):
            position, _ = locate(plan_ref, group, jnp.bitwise_xor(group, 1) * OWN + slot, home)
            copy = pltpu.make_async_copy(b_hbm.at[position], out_ref.at[slot], sem.at[slot])
            copy.start()
            copies.append(copy)
        for copy in copies:
            copy.wait()

    return pl.pallas_call(
        kernel,
        out_shape=jax.ShapeDtypeStruct((OWN, rows, width), jnp.float32),
        in_specs=[SMEM, HBM],
        out_specs=VMEM,
        scratch_shapes=[pltpu.SemaphoreType.DMA((OWN,))],
        compiler_params=PARAMS,
        name="stiff_out",
    )(plan, stiff)


def stiff_merge(plan, stiff, arrived):
    home, rows, width = stiff.shape

    def kernel(plan_ref, b_hbm, arrived_ref, out_ref, sem):
        group = lax.axis_index("group")
        for slot in range(OWN):
            position, here = locate(plan_ref, group, group * OWN + slot, home)

            @pl.when(here)
            def _():
                copy = pltpu.make_async_copy(b_hbm.at[position], out_ref.at[slot], sem.at[slot])
                copy.start()
                copy.wait()

            @pl.when(jnp.logical_not(here))
            def _():
                out_ref[slot] = arrived_ref[slot]

    return pl.pallas_call(
        kernel,
        out_shape=jax.ShapeDtypeStruct((OWN, rows, width), jnp.float32),
        in_specs=[SMEM, HBM, VMEM],
        out_specs=VMEM,
        scratch_shapes=[pltpu.SemaphoreType.DMA((OWN,))],
        compiler_params=PARAMS,
        name="stiff_merge",
    )(plan, stiff, arrived)


def split(value):
    high = value.astype(jnp.bfloat16)
    return high, (value - high.astype(jnp.float32)).astype(jnp.bfloat16)


def add_chunks(total_ref, chunks, start):
    for packet, places, piece in chunks:
        c_high, c_low = split(piece)
        left = jnp.concatenate([c_high, c_high, c_low], axis=0)
        for n in range(0, len(places), 2):
            x = jnp.concatenate([packet[places[n]], packet[places[n + 1]]], axis=1)
            x_high, x_low = split(x)
            right = jnp.concatenate([x_high, x_low, x_high], axis=0)
            product = lax.dot_general(left, right, (((0,), (0,)), ((), ())), preferred_element_type=jnp.float32)
            where = (slice(None), pl.ds(n * LANES, 2 * LANES))
            total_ref[where] = product if start else total_ref[where] + product
        start = False


def gathered(sources):
    arrays, layout = [], []

    def place(array):
        for k, known in enumerate(arrays):
            if known is array:
                return k
        arrays.append(array)
        return len(arrays) - 1

    for packet, places, holder, index in sources:
        layout.append((place(packet), places, place(holder), index))
    return arrays, layout


def chunks_of(refs, layout):
    return [
        (refs[k], places, refs[holder][...] if index is None else refs[holder][index])
        for k, places, holder, index in layout
    ]


def accumulate(total, sources, width, name):
    arrays, layout = gathered(sources)
    given = [] if total is None else [total]
    n_given = len(given)

    def kernel(*refs):
        total_ref = refs[-1]
        if n_given:
            total_ref[...] = refs[0][...]
        add_chunks(total_ref, chunks_of(refs[n_given:-1], layout), not n_given)

    return pl.pallas_call(
        kernel,
        out_shape=jax.ShapeDtypeStruct((LANES, width), jnp.float32),
        in_specs=[VMEM] * (n_given + len(arrays)),
        out_specs=VMEM,
        input_output_aliases={0: 0} if n_given else {},
        compiler_params=PARAMS,
        cost_estimate=pl.CostEstimate(flops=2 * 144 * 128 * 1024, bytes_accessed=1 << 20, transcendentals=0),
        name=name,
    )(*given, *arrays)


def last_chunks(total, sources):
    rows, width = LANES // 2, total.shape[1]
    arrays, layout = gathered(sources)

    def kernel(total_ref, *refs):
        send_ref, keep_ref, sum_ref = refs[-3:]
        sum_ref[...] = total_ref[...]
        add_chunks(sum_ref, chunks_of(refs[:-3], layout), False)
        mine = lax.axis_index("tile_0")
        send_ref[...] = sum_ref[pl.ds(pl.multiple_of((1 - mine) * rows, rows), rows), :]
        keep_ref[...] = sum_ref[pl.ds(pl.multiple_of(mine * rows, rows), rows), :]

    half = jax.ShapeDtypeStruct((rows, width), jnp.float32)
    return pl.pallas_call(
        kernel,
        out_shape=(half, half),
        in_specs=[VMEM] * (1 + len(arrays)),
        out_specs=(VMEM, VMEM),
        scratch_shapes=[pltpu.VMEM((LANES, width), jnp.float32)],
        compiler_params=PARAMS,
        name="last_chunks",
    )(total, *arrays)


def finish(result, stiff, product, chain):
    rows, width = product.shape
    given = [] if result is None else [result]

    def kernel(*refs):
        stiff_ref, product_ref, out_hbm, buf, sem = refs[len(given) :]
        slot = slot_of(chain)
        buf[...] = stiff_ref[slot] - product_ref[...]
        copy = pltpu.make_async_copy(buf, out_hbm.at[slot], sem)
        copy.start()
        copy.wait()

    return pl.pallas_call(
        kernel,
        out_shape=jax.ShapeDtypeStruct((OWN, rows, width), jnp.float32),
        in_specs=[HBM] * len(given) + [VMEM, VMEM],
        out_specs=HBM,
        scratch_shapes=[pltpu.VMEM((rows, width), jnp.float32), pltpu.SemaphoreType.DMA],
        input_output_aliases={0: 0} if given else {},
        compiler_params=PARAMS,
        name=f"finish_{chain}",
    )(*given, stiff, product)


def shifted(array, axis, distance):
    size = lax.axis_size(axis)
    return lax.ppermute(array, axis, [(i, (i + distance) % size) for i in range(size)])


def swapped(array, axis):
    return lax.ppermute(array, axis, [(i, i ^ 1) for i in range(lax.axis_size(axis))])


def crossed(array, distance):
    size = lax.axis_size("tile_1")
    pairs = [(x * size + z, (1 - x) * size + (z + distance) % size) for x in range(2) for z in range(size)]
    return lax.ppermute(array, TILE, pairs)


def body(coupling, interior_solve, boundary_stiffness, migration):
    home, depth, width = interior_solve.shape
    blocks = width // LANES
    pieces = jnp.swapaxes(coupling, 1, 2)
    in_hbm = [pltpu.with_memory_space_constraint(a, pltpu.HBM) for a in (migration, pieces, interior_solve)]
    outgoing = pack(*in_hbm, True)
    arrived = [swapped(outgoing[0], "group"), swapped(outgoing[1], "group")]
    local = pack(*in_hbm, False)
    ups, downs, owns = [None, None], [None, None], [None, None]
    for chain in range(2):
        ups[chain], downs[chain], owns[chain] = merge(outgoing[2], arrived[chain], local[chain], chain)
    stiff_arrived = swapped(stiff_out(migration, boundary_stiffness), "group")
    stiff = stiff_merge(migration, boundary_stiffness, stiff_arrived)

    def run(first):
        return list(range(first, first + blocks))

    crossed_own = crossed(owns[1], 0)
    sources = [(ups[0], run(hops(0)[0]), owns[0], 0)]
    total = None
    for step in range(1, 4):
        for chain in range(2):
            if step == 1 and chain == 1:
                ups[chain], downs[chain] = crossed(ups[chain], 1), crossed(downs[chain], -1)
            else:
                sent_up = ups[chain] if step == 1 else ups[chain][1:]
                sent_down = downs[chain] if step == 1 else downs[chain][:-1]
                ups[chain], downs[chain] = shifted(sent_up, "tile_1", 1), shifted(sent_down, "tile_1", -1)
        total = accumulate(total, sources, width, f"chunks_{step}")
        sources = [] if step > 1 else [(crossed_own, run(0), crossed_own, blocks)]
        for chain in range(2):
            left_up, left_down = hops(chain)[0] - step, hops(chain)[1] - step
            sources.append((ups[chain], run(left_up + 1), ups[chain], 0))
            sources.append((downs[chain], run(0), downs[chain], blocks + left_down))
    far0, far1 = shifted(downs[0][:-1], "tile_1", -1), shifted(ups[1][1:], "tile_1", 1)
    total = accumulate(total, sources, width, "chunks_4")
    send, keep = last_chunks(total, [(far0, run(0), far0, blocks), (far1, run(1), far1, 0)])
    other = swapped(send, "tile_0")
    return finish(finish(None, stiff, keep, 0), stiff, other, 1)


def solution(mesh):
    finer = Mesh(mesh.devices.reshape(mesh.shape["group"], 2, 8), ("group", "tile_0", "tile_1"))
    in_specs = (P("group", None, TILE), P("group", TILE, None), P("group", TILE, None), P())
    out_specs = P("group", TILE, None)
    return jax.shard_map(body, mesh=finer, in_specs=in_specs, out_specs=out_specs, check_vma=False)
```

```python
import jax
import jax.numpy as jnp
from jax import lax
from jax.experimental import pallas as pl
from jax.experimental.pallas import tpu as pltpu
from jax.sharding import Mesh
from jax.sharding import PartitionSpec as P

OWN = 2
TILE = ("tile_0", "tile_1")
LANES = 128
PARAMS = pltpu.CompilerParams(vmem_limit_bytes=32 * 1024 * 1024)
SMEM = pl.BlockSpec(memory_space=pltpu.SMEM)
VMEM = pl.BlockSpec(memory_space=pltpu.VMEM)
HBM = pl.BlockSpec(memory_space=pltpu.HBM)


def hops(chain):
    return (3, 4) if chain == 0 else (4, 3)


def slot_of(chain):
    column = lax.axis_index("tile_0")
    return column if chain == 0 else 1 - column


def locate(plan, group, wanted, home):
    position, here = jnp.int32(0), jnp.bool_(False)
    for k in range(home):
        match = plan[group * home + k] == wanted
        position = jnp.where(match, jnp.int32(k), position)
        here = jnp.logical_or(here, match)
    return position, here


def pack(plan, coupling, solve, for_partner):
    home, depth, width = solve.shape
    blocks = width // LANES

    def kernel(plan_hbm, c_hbm, x_hbm, out0, out1, *refs):
        plan_ref, c_buf, x_buf, plan_sem, c_sem, x_sem = refs[-6:]
        group = lax.axis_index("group")
        place = lax.axis_index("tile_1")
        owner = jnp.bitwise_xor(group, 1) if for_partner else group
        outs = (out0, out1)
        copies = [
            pltpu.make_async_copy(plan_hbm, plan_ref, plan_sem),
            pltpu.make_async_copy(c_hbm, c_buf, c_sem),
            pltpu.make_async_copy(x_hbm, x_buf, x_sem),
        ]
        for copy in copies:
            copy.start()
        low = lax.broadcasted_iota(jnp.int32, (depth, LANES), 1) < LANES // 2
        copies[0].wait()
        positions = [locate(plan_ref, group, owner * OWN + slot_of(slot), home)[0] for slot in range(OWN)]
        if for_partner:
            for chain in range(2):
                _, here = locate(plan_ref, group, group * OWN + slot_of(chain), home)
                refs[0][chain] = jnp.broadcast_to(here.astype(jnp.int32), refs[0].shape[1:])
        copies[1].wait()
        for slot in range(OWN):
            up = hops(slot)[0]
            for m in range(blocks // 2):
                first = c_buf[positions[slot], :, pl.ds(m * LANES, LANES)]
                second = c_buf[positions[slot], :, pl.ds((m + blocks // 2) * LANES, LANES)]
                even = jnp.where(low, first, pltpu.roll(second, LANES // 2, 1))
                odd = jnp.where(low, pltpu.roll(first, LANES // 2, 1), second)
                for to, piece in ((2 * m, even), (2 * m + 1, odd)):
                    ahead = jnp.bitwise_and(to - place, blocks - 1)
                    spot = jnp.where(ahead == 0, 15, jnp.where(ahead <= up, ahead - 1, ahead + 7))
                    outs[slot][spot] = piece
        copies[2].wait()
        for slot in range(OWN):
            up = hops(slot)[0]
            for n in range(blocks):
                outs[slot][up + n] = x_buf[positions[slot], :, pl.ds(n * LANES, LANES)]

    packet = jax.ShapeDtypeStruct((2 * blocks, depth, LANES), jnp.float32)
    return pl.pallas_call(
        kernel,
        out_shape=(packet, packet) + ((jax.ShapeDtypeStruct((2, 8, LANES), jnp.int32),) if for_partner else ()),
        in_specs=[HBM] * 3,
        out_specs=(VMEM, VMEM) + ((VMEM,) if for_partner else ()),
        scratch_shapes=[
            pltpu.SMEM(plan.shape, jnp.int32),
            pltpu.VMEM((home, depth, width), jnp.float32),
            pltpu.VMEM((home, depth, width), jnp.float32),
            pltpu.SemaphoreType.DMA,
            pltpu.SemaphoreType.DMA,
            pltpu.SemaphoreType.DMA,
        ],
        compiler_params=PARAMS,
        name="pack_partner" if for_partner else "pack_own",
    )(plan, coupling, solve)


def merge(at_home, arrived, local, chain):
    total, depth, _ = arrived.shape
    up, down = hops(chain)
    blocks = total // 2

    def kernel(home_ref, arrived_ref, local_ref, up_ref, down_ref, own_ref):
        here = jnp.broadcast_to(home_ref[chain, 0:1, :], (depth, LANES)) != 0
        for k in range(total):
            block = jnp.where(here, local_ref[k], arrived_ref[k])
            if k < up + blocks:
                up_ref[k] = block
            if up <= k < total - 1:
                down_ref[k - up] = block
            if chain == 1 and up <= k < up + blocks:
                own_ref[k - up] = block
            if k == total - 1:
                own_ref[blocks if chain else 0] = block

    return pl.pallas_call(
        kernel,
        out_shape=(
            jax.ShapeDtypeStruct((up + blocks, depth, LANES), jnp.float32),
            jax.ShapeDtypeStruct((down + blocks, depth, LANES), jnp.float32),
            jax.ShapeDtypeStruct((1 if chain == 0 else 1 + blocks, depth, LANES), jnp.float32),
        ),
        in_specs=[VMEM, VMEM, VMEM],
        out_specs=(VMEM, VMEM, VMEM),
        compiler_params=PARAMS,
        name=f"merge_{chain}",
    )(at_home, arrived, local)


def pack_stiff(plan, stiff):
    home, rows, width = stiff.shape

    def kernel(plan_hbm, b_hbm, leaving_ref, own_ref, plan_ref, plan_sem, sem):
        group = lax.axis_index("group")
        plan_copy = pltpu.make_async_copy(plan_hbm, plan_ref, plan_sem)
        plan_copy.start()
        plan_copy.wait()
        copies = []
        for k, (owner, out_ref) in enumerate(((jnp.bitwise_xor(group, 1), leaving_ref), (group, own_ref))):
            for slot in range(OWN):
                position, _ = locate(plan_ref, group, owner * OWN + slot, home)
                copies.append(pltpu.make_async_copy(b_hbm.at[position], out_ref.at[slot], sem.at[k, slot]))
        for copy in copies:
            copy.start()
        for copy in copies:
            copy.wait()

    half = jax.ShapeDtypeStruct((OWN, rows, width), jnp.float32)
    return pl.pallas_call(
        kernel,
        out_shape=(half, half),
        in_specs=[HBM, HBM],
        out_specs=(VMEM, VMEM),
        scratch_shapes=[
            pltpu.SMEM(plan.shape, jnp.int32),
            pltpu.SemaphoreType.DMA,
            pltpu.SemaphoreType.DMA((2, OWN)),
        ],
        compiler_params=PARAMS,
        name="pack_stiff",
    )(plan, stiff)


def split(value):
    high = value.astype(jnp.bfloat16)
    return high, (value - high.astype(jnp.float32)).astype(jnp.bfloat16)


def add_chunks(total_ref, chunks, start):
    for packet, places, piece in chunks:
        c_high, c_low = split(piece)
        left = jnp.concatenate([c_high, c_high, c_low], axis=0)
        for n in range(0, len(places), 2):
            x = jnp.concatenate([packet[places[n]], packet[places[n + 1]]], axis=1)
            x_high, x_low = split(x)
            right = jnp.concatenate([x_high, x_low, x_high], axis=0)
            product = lax.dot_general(left, right, (((0,), (0,)), ((), ())), preferred_element_type=jnp.float32)
            where = (slice(None), pl.ds(n * LANES, 2 * LANES))
            total_ref[where] = product if start else total_ref[where] + product
        start = False


def gathered(sources):
    arrays, layout = [], []

    def place(array):
        for k, known in enumerate(arrays):
            if known is array:
                return k
        arrays.append(array)
        return len(arrays) - 1

    for packet, places, holder, index in sources:
        layout.append((place(packet), places, place(holder), index))
    return arrays, layout


def chunks_of(refs, layout):
    return [
        (refs[k], places, refs[holder][...] if index is None else refs[holder][index])
        for k, places, holder, index in layout
    ]


def accumulate(total, sources, width, name):
    arrays, layout = gathered(sources)
    given = [] if total is None else [total]
    n_given = len(given)

    def kernel(*refs):
        total_ref = refs[-1]
        if n_given:
            total_ref[...] = refs[0][...]
        add_chunks(total_ref, chunks_of(refs[n_given:-1], layout), not n_given)

    return pl.pallas_call(
        kernel,
        out_shape=jax.ShapeDtypeStruct((LANES, width), jnp.float32),
        in_specs=[VMEM] * (n_given + len(arrays)),
        out_specs=VMEM,
        input_output_aliases={0: 0} if n_given else {},
        compiler_params=PARAMS,
        cost_estimate=pl.CostEstimate(flops=2 * 144 * 128 * 1024, bytes_accessed=1 << 20, transcendentals=0),
        name=name,
    )(*given, *arrays)


def last_chunks(total, sources):
    rows, width = LANES // 2, total.shape[1]
    arrays, layout = gathered(sources)

    def kernel(total_ref, *refs):
        send_ref, keep_ref, sum_ref = refs[-3:]
        sum_ref[...] = total_ref[...]
        add_chunks(sum_ref, chunks_of(refs[:-3], layout), False)
        mine = lax.axis_index("tile_0")
        send_ref[...] = sum_ref[pl.ds(pl.multiple_of((1 - mine) * rows, rows), rows), :]
        keep_ref[...] = sum_ref[pl.ds(pl.multiple_of(mine * rows, rows), rows), :]

    half = jax.ShapeDtypeStruct((rows, width), jnp.float32)
    return pl.pallas_call(
        kernel,
        out_shape=(half, half),
        in_specs=[VMEM] * (1 + len(arrays)),
        out_specs=(VMEM, VMEM),
        scratch_shapes=[pltpu.VMEM((LANES, width), jnp.float32)],
        compiler_params=PARAMS,
        name="last_chunks",
    )(total, *arrays)


def finish(result, at_home, stiff_own, stiff_arrived, product, chain):
    rows, width = product.shape
    given = [] if result is None else [result]

    def kernel(*refs):
        home_ref, own_ref, arrived_ref, product_ref, out_hbm, buf, sem = refs[len(given) :]
        slot = slot_of(chain)
        for n in range(0, width, LANES):
            columns = pl.ds(n, LANES)
            here = jnp.broadcast_to(home_ref[chain, 0:1, :], (rows, LANES)) != 0
            stiff = jnp.where(here, own_ref[slot, :, columns], arrived_ref[slot, :, columns])
            buf[:, columns] = stiff - product_ref[:, columns]
        copy = pltpu.make_async_copy(buf, out_hbm.at[slot], sem)
        copy.start()
        copy.wait()

    return pl.pallas_call(
        kernel,
        out_shape=jax.ShapeDtypeStruct((OWN, rows, width), jnp.float32),
        in_specs=[HBM] * len(given) + [VMEM] * 4,
        out_specs=HBM,
        scratch_shapes=[pltpu.VMEM((rows, width), jnp.float32), pltpu.SemaphoreType.DMA],
        input_output_aliases={0: 0} if given else {},
        compiler_params=PARAMS,
        name=f"finish_{chain}",
    )(*given, at_home, stiff_own, stiff_arrived, product)


def after(array, *earlier):
    return lax.optimization_barrier((array, *earlier))[0]


def shifted(array, axis, distance):
    size = lax.axis_size(axis)
    return lax.ppermute(array, axis, [(i, (i + distance) % size) for i in range(size)])


def swapped(array, axis):
    return lax.ppermute(array, axis, [(i, i ^ 1) for i in range(lax.axis_size(axis))])


def crossed(array, distance):
    size = lax.axis_size("tile_1")
    pairs = [(x * size + z, (1 - x) * size + (z + distance) % size) for x in range(2) for z in range(size)]
    return lax.ppermute(array, TILE, pairs)


def body(coupling, interior_solve, boundary_stiffness, migration):
    home, depth, width = interior_solve.shape
    blocks = width // LANES
    pieces = jnp.swapaxes(coupling, 1, 2)
    in_hbm = [pltpu.with_memory_space_constraint(a, pltpu.HBM) for a in (migration, pieces, interior_solve)]
    outgoing = pack(*in_hbm, True)
    arrived = [swapped(outgoing[0], "group"), swapped(outgoing[1], "group")]
    local = pack(*in_hbm, False)
    ups, downs, owns = [None, None], [None, None], [None, None]
    for chain in range(2):
        ups[chain], downs[chain], owns[chain] = merge(outgoing[2], arrived[chain], local[chain], chain)
    stiff_leaving, stiff_own = pack_stiff(
        after(in_hbm[0], ups[1]), pltpu.with_memory_space_constraint(boundary_stiffness, pltpu.HBM)
    )
    stiff_arrived = swapped(stiff_leaving, "group")

    def run(first):
        return list(range(first, first + blocks))

    crossed_own = crossed(owns[1], 0)
    sources = [(ups[0], run(hops(0)[0]), owns[0], 0)]
    total = None
    for step in range(1, 4):
        for chain in range(2):
            if step == 1 and chain == 1:
                ups[chain], downs[chain] = crossed(ups[chain], 1), crossed(downs[chain], -1)
            else:
                sent_up = ups[chain] if step == 1 else ups[chain][1:]
                if step == 2 and chain == 0:
                    sent_up = after(sent_up, stiff_leaving)
                sent_down = downs[chain] if step == 1 else downs[chain][:-1]
                ups[chain], downs[chain] = shifted(sent_up, "tile_1", 1), shifted(sent_down, "tile_1", -1)
        total = accumulate(total, sources, width, f"chunks_{step}")
        sources = [] if step > 1 else [(crossed_own, run(0), crossed_own, blocks)]
        for chain in range(2):
            left_up, left_down = hops(chain)[0] - step, hops(chain)[1] - step
            sources.append((ups[chain], run(left_up + 1), ups[chain], 0))
            sources.append((downs[chain], run(0), downs[chain], blocks + left_down))
    far0, far1 = shifted(downs[0][:-1], "tile_1", -1), shifted(ups[1][1:], "tile_1", 1)
    total = accumulate(total, sources, width, "chunks_4")
    send, keep = last_chunks(total, [(far0, run(0), far0, blocks), (far1, run(1), far1, 0)])
    other = swapped(send, "tile_0")
    result = finish(None, outgoing[2], stiff_own, stiff_arrived, keep, 0)
    return finish(result, outgoing[2], stiff_own, stiff_arrived, other, 1)


def solution(mesh):
    finer = Mesh(mesh.devices.reshape(mesh.shape["group"], 2, 8), ("group", "tile_0", "tile_1"))
    in_specs = (P("group", None, TILE), P("group", TILE, None), P("group", TILE, None), P())
    out_specs = P("group", TILE, None)
    return jax.shard_map(body, mesh=finer, in_specs=in_specs, out_specs=out_specs, check_vma=False)
```
